1024 devices in a mesh: gx: 4 (over x), gy: 16 (over z_hi, y), gz: 16 (over z_lo, core).
Axes of the slice: x: 4, y: 8, z: 16 (z_hi: 2, z_lo: 8; z = z_hi * 8 + z_lo), core: 2. Of those that a mesh axis runs over, the one named last changes fastest.
Arguments:
- populations: float32 [19, 8, 256, 2048], P(None, 'gx', 'gy', 'gz'), may hold values from 0.1 to 12, as said below
- shear_rate: float32 [8, 256, 2048], P('gx', 'gy', 'gz'), may hold values from 1 to 1.9
- part_cell: int32 [8388608], P(('gx', 'gy', 'gz')), may hold values from 0 to 4095
- part_move: int32 [8388608], P(('gx', 'gy', 'gz')), may hold values from 0 to 6
- part_mask: int32 [8388608], P(('gx', 'gy', 'gz')), may hold values 0 or 1
- part_velocity: float32 [3, 8388608], P(None, ('gx', 'gy', 'gz')), may hold values from -6 to 6
- part_mass: float32 [8388608], P(('gx', 'gy', 'gz')), may hold values from 0.5 to 2
Outputs:
- populations_out: float32 [19, 8, 256, 2048], P(None, 'gx', 'gy', 'gz')
- sources: float32 [4, 8, 256, 2048], P(None, 'gx', 'gy', 'gz')
- velocity_out: float32 [3, 8388608], P(None, ('gx', 'gy', 'gz'))
The draws below stay inside these ranges and needn't reach their ends.
Inputs may be any that keep to these rules, and one draw needn't show every extreme that they name: `populations`: each entry is a positive population; a node's 19 values sum to its density. `part_cell`: local index of the particle's cell in the brick of the device holding it, (x * 16 + y) * 128 + z. `part_move`: 0 stays; 1 and 2 move to the next node along +x and -x, 3 and 4 along +y and -y, 5 and 6 along +z and -z. `part_mask`: 1 marks a particle of the advanced subset.
All inputs are finite; a program needn't handle non-finite values. No bound on the sum of `part_mask` on one device may be relied on, other than what follows from the above.
Results may differ from the reference program's by a relative error of at most 0.0001.
Values sent between devices are 32-bit elements; how exact they have to be, the bound alone decides.
No kernel may reach another device: no remote copies, remote signals or barrier semaphores. Data moves between devices by JAX's collectives and lax.ppermute only.
A program may use at most 32 MiB of HBM per device.

```python
import math
import jax
import jax.numpy as jnp
import numpy as np
from jax import lax

BX = 2
BY = 16
BZ = 128
PART_DEV = 8192
NX = 8
NY = 256
NZ = 2048
NP = 8388608
N_GY = 16
N_GZ = 16


def draw_populations(key, part):
    weights = jnp.array([1.0 / 3.0] + [1.0 / 18.0] * 6 + [1.0 / 36.0] * 12, jnp.float32)
    spread = jax.random.uniform(key, (19, NX, NY, NZ), jnp.float32, 0.3, 1.7)
    return 20.0 * weights[:, None, None, None] * spread


def place_ends(values, stream_key, low, high):
    dims = values.shape
    spot = [jax.random.randint(jax.random.fold_in(stream_key, axis), (), 0, dims[axis]) for axis in range(len(dims))]
    values = values.at[tuple(spot)].set(low)
    longest = dims.index(max(dims))
    spot[longest] = (spot[longest] + 1) % dims[longest]
    return values.at[tuple(spot)].set(high)


def steps_of(stream_key, shape, shards, least, largest):
    factor_of, own = 1.0, jax.random.fold_in(stream_key, 6)
    for position, shards_of in shards:
        heights = jnp.exp(jax.random.uniform(jax.random.fold_in(own, position), (shards_of,), jnp.float32, least / len(shards), largest / len(shards)))
        factor_of = factor_of * jnp.repeat(heights, shape[position] // shards_of).reshape([-1 if axis == position else 1 for axis in range(len(shape))])
    return factor_of


def bell_draw(stream_key, extent, scale, bound, shards=(), kind=jnp.bfloat16):
    values = jax.random.normal(stream_key, extent, jnp.float32) * scale
    if len(shards) > 0:
        values = steps_of(stream_key, extent, shards, -0.22, 0.18) * values
    return jnp.clip(values, min=-bound, max=bound).astype(kind)


def setup_inputs(seed: int = 0) -> dict:
    keys = jax.random.split(jax.random.key(seed), 8)
    return {
        "populations": draw_populations(jax.random.fold_in(keys[7], 71), 0),
        "shear_rate": jnp.clip(jnp.exp(math.log(1.9) - 0.64185387 * jax.random.uniform(keys[1], (NX, NY, NZ), jnp.float32) ** steps_of(keys[1], (NX, NY, NZ), ((0, 4), (1, 16), (2, 16)), -0.2, 0.2)), 1.0, 1.9),
        "part_cell": place_ends(jax.random.randint(keys[2], (NP,), 0, BX * BY * BZ), jax.random.fold_in(keys[2], 1), 0, (BX * BY * BZ) - 1).astype(jnp.int32),
        "part_move": place_ends(jax.random.randint(keys[3], (NP,), 0, 7), jax.random.fold_in(keys[3], 1), 0, 6).astype(jnp.int32),
        "part_mask": place_ends((jax.random.randint(keys[4], (NP,), 0, 4) < 3).astype(jnp.int32), jax.random.fold_in(keys[4], 1), 0, 1),
        "part_velocity": bell_draw(keys[5], (3, NP), 1.0, 6.0, ((1, 1024),), jnp.float32),
        "part_mass": jnp.clip(jnp.exp(math.log(2.0) - 1.3862944 * jax.random.uniform(keys[6], (NP,), jnp.float32) ** steps_of(keys[6], (NP,), ((0, 1024),), -0.2, 0.2)), 0.5, 2.0),
    }


drag_factor = 0.5

def lattice_tables():
    speeds = np.array([[0, 0, 0], [1, 0, 0], [-1, 0, 0], [0, 1, 0], [0, -1, 0], [0, 0, 1], [0, 0, -1], [1, 1, 0], [-1, -1, 0], [1, -1, 0], [-1, 1, 0], [1, 0, 1], [-1, 0, -1], [1, 0, -1], [-1, 0, 1], [0, 1, 1], [0, -1, -1], [0, 1, -1], [0, -1, 1]])
    comp_x = speeds[:, 0]
    comp_y = speeds[:, 1]
    comp_z = speeds[:, 2]
    square = comp_x * comp_x + comp_y * comp_y + comp_z * comp_z
    polynomials = [np.ones(19), 19.0 * square - 30.0, (21.0 * square * square - 53.0 * square + 24.0) / 2.0, comp_x, (5.0 * square - 9.0) * comp_x, comp_y, (5.0 * square - 9.0) * comp_y, comp_z, (5.0 * square - 9.0) * comp_z, 3.0 * comp_x * comp_x - square, (3.0 * square - 5.0) * (3.0 * comp_x * comp_x - square), comp_y * comp_y - comp_z * comp_z, (3.0 * square - 5.0) * (comp_y * comp_y - comp_z * comp_z), comp_x * comp_y, comp_y * comp_z, comp_x * comp_z, comp_x * (comp_y * comp_y - comp_z * comp_z), comp_y * (comp_z * comp_z - comp_x * comp_x), comp_z * (comp_x * comp_x - comp_y * comp_y)]
    basis = np.stack(polynomials)
    basis = basis / np.sqrt(np.sum(basis * basis, axis=1, keepdims=True))
    fixed_rates = np.array([0.0, 1.19, 1.4, 0.0, 1.2, 0.0, 1.2, 0.0, 1.2, 0.0, 1.4, 0.0, 1.4, 0.0, 0.0, 0.0, 1.98, 1.98, 1.98])
    shear_rows = np.zeros(19)
    shear_rows[[9, 11, 13, 14, 15]] = 1.0
    weights = np.array([1.0 / 3.0] + [1.0 / 18.0] * 6 + [1.0 / 36.0] * 12)
    return (speeds, basis, fixed_rates, shear_rows, weights)

def fluid_velocity(distribution):
    speeds = lattice_tables()[0]
    lattice_vel = jnp.asarray(speeds, jnp.float32)
    density = lax.optimization_barrier(jnp.sum(distribution, axis=0))
    momentum = jnp.dot(lattice_vel.T, distribution, precision=lax.Precision.HIGHEST)
    return momentum / density

def collide_flat(distribution, shear_field):
    speeds, basis, fixed_rates, shear_rows, weights = lattice_tables()
    lattice_vel = jnp.asarray(speeds, jnp.float32)
    basis_mat = jnp.asarray(basis, jnp.float32)
    fixed_vec = jnp.asarray(fixed_rates, jnp.float32)
    shear_vec = jnp.asarray(shear_rows, jnp.float32)
    weight_vec = jnp.asarray(weights, jnp.float32)
    density = lax.optimization_barrier(jnp.sum(distribution, axis=0))
    momentum = jnp.dot(lattice_vel.T, distribution, precision=lax.Precision.HIGHEST)
    velocity = momentum / density
    projected = jnp.dot(lattice_vel, velocity, precision=lax.Precision.HIGHEST)
    speed_sq = lax.optimization_barrier(jnp.sum(velocity * velocity, axis=0))
    equilibrium = weight_vec[:, None] * density * (1.0 + 3.0 * projected + 4.5 * projected * projected - 1.5 * speed_sq)
    moments = jnp.dot(basis_mat, distribution - equilibrium, precision=lax.Precision.HIGHEST)
    relax_rates = fixed_vec[:, None] + shear_vec[:, None] * shear_field[None, :]
    return distribution - jnp.dot(basis_mat.T, relax_rates * moments, precision=lax.Precision.HIGHEST)

def reference(populations, shear_rate, part_cell, part_move, part_mask, part_velocity, part_mass):
    speeds = lattice_tables()[0]
    current = populations
    shear_flat = shear_rate.reshape(-1)
    for sweep_index in range(2):
        collided = collide_flat(current.reshape(19, -1), shear_flat).reshape(populations.shape)
        current = jnp.stack([jnp.roll(collided[direction], (int(speeds[direction, 0]), int(speeds[direction, 1]), int(speeds[direction, 2])), axis=(0, 1, 2)) for direction in range(19)])
    velocity_field = fluid_velocity(current.reshape(19, -1)).reshape(3, NX, NY, NZ)
    particle = jnp.arange(NP, dtype=jnp.int32)
    device = particle // PART_DEV
    index_x = device // (N_GY * N_GZ)
    index_y = device // N_GZ % N_GY
    index_z = device % N_GZ
    local_x = part_cell // (BY * BZ)
    local_y = part_cell // BZ % BY
    local_z = part_cell % BZ
    global_x = index_x * BX + local_x
    global_y = index_y * BY + local_y
    global_z = index_z * BZ + local_z
    sampled = velocity_field[:, global_x, global_y, global_z]
    active = part_mask.astype(jnp.float32)
    new_velocity = part_velocity + drag_factor * active * (sampled - part_velocity)
    payload = jnp.concatenate([part_mass * (part_velocity - new_velocity), (part_mass * active)[None]], 0)
    offset_x = (part_move == 1).astype(jnp.int32) - (part_move == 2).astype(jnp.int32)
    offset_y = (part_move == 3).astype(jnp.int32) - (part_move == 4).astype(jnp.int32)
    offset_z = (part_move == 5).astype(jnp.int32) - (part_move == 6).astype(jnp.int32)
    target = ((global_x + offset_x) % NX * NY + (global_y + offset_y) % NY) * NZ + (global_z + offset_z) % NZ
    sources = jnp.zeros((4, NX * NY * NZ), jnp.float32).at[:, target].add(payload).reshape(4, NX, NY, NZ)
    return (current, sources, new_velocity)
```

```python
import jax
import jax.numpy as jnp
from jax import lax
from jax.experimental import pallas as pl
from jax.experimental.pallas import tpu as pltpu
from jax.sharding import PartitionSpec as P

SPEEDS = (
    (0, 0, 0),
    (1, 0, 0),
    (-1, 0, 0),
    (0, 1, 0),
    (0, -1, 0),
    (0, 0, 1),
    (0, 0, -1),
    (1, 1, 0),
    (-1, -1, 0),
    (1, -1, 0),
    (-1, 1, 0),
    (1, 0, 1),
    (-1, 0, -1),
    (1, 0, -1),
    (-1, 0, 1),
    (0, 1, 1),
    (0, -1, -1),
    (0, 1, -1),
    (0, -1, 1),
)
SHEAR = 19
UP = [i for i in range(19) if SPEEDS[i][0] == 1]
FLAT = [i for i in range(19) if SPEEDS[i][0] == 0]
DOWN = [i for i in range(19) if SPEEDS[i][0] == -1]
X_LOW = [(f, -1) for f in UP + FLAT + [SHEAR]] + [(f, -2) for f in UP]
X_HIGH = [(f, 2) for f in DOWN + FLAT + [SHEAR]] + [(f, 3) for f in DOWN]
PAIRS = X_LOW + [(f, 0) for f in range(20)] + [(f, 1) for f in range(20)] + X_HIGH
INDEX = {pair: q for q, pair in enumerate(PAIRS)}
FIRST = 42
DEP_LANE = 3 * (len(PAIRS) - FIRST)
Y_ROWS = 264
VMEM = pl.BlockSpec(memory_space=pltpu.VMEM)
SMEM = pl.BlockSpec(memory_space=pltpu.SMEM)


def relax(f, shear):
    s1, s2, s3 = f[1] + f[2], f[3] + f[4], f[5] + f[6]
    d1, d2, d3 = f[1] - f[2], f[3] - f[4], f[5] - f[6]
    e1, e2, e3 = f[7] + f[8], f[9] + f[10], f[11] + f[12]
    e4, e5, e6 = f[13] + f[14], f[15] + f[16], f[17] + f[18]
    g1, g2, g3 = f[7] - f[8], f[9] - f[10], f[11] - f[12]
    g4, g5, g6 = f[13] - f[14], f[15] - f[16], f[17] - f[18]
    exy, exz, eyz = e1 + e2, e3 + e4, e5 + e6
    s23, m23 = s2 + s3, s2 - s3
    axes = s1 + s23
    exx = exy + exz
    edges = exx + eyz
    rho = f[0] + axes + edges
    gp, gm = g1 + g2, g1 - g2
    hp, hm = g3 + g4, g3 - g4
    kp, km = g5 + g6, g5 - g6
    gx, gy, gz = gp + hp, gm + kp, hm + km
    jx, jy, jz = d1 + gx, d2 + gy, d3 + gz
    inv = 1.0 / rho
    ux, uy, uz = jx * inv, jy * inv, jz * inv
    xx, yy, zz = jx * ux, jy * uy, jz * uz
    sq = xx + yy + zz
    n1 = 8.0 * edges - 11.0 * axes - 30.0 * f[0] + (11.0 * rho - 19.0 * sq)
    n2 = 12.0 * f[0] - 4.0 * axes + edges - (3.0 * rho - 5.5 * sq)
    a9 = 2.0 * s1 - s23
    b9 = exx - 2.0 * eyz
    q9 = 3.0 * xx - sq
    b11 = exy - exz
    q11 = yy - zz
    t1 = n1 * (1.19 / 2394.0)
    t2 = n2 * (1.4 / 252.0)
    t4 = (gx - 4.0 * d1 + (2.0 / 3.0) * jx) * (1.2 / 40.0)
    t6 = (gy - 4.0 * d2 + (2.0 / 3.0) * jy) * (1.2 / 40.0)
    t8 = (gz - 4.0 * d3 + (2.0 / 3.0) * jz) * (1.2 / 40.0)
    t9 = (a9 + b9 - q9) * (shear * (1.0 / 36.0))
    t10 = (b9 - 2.0 * a9 + 0.5 * q9) * (1.4 / 72.0)
    t11 = (m23 + b11 - q11) * (shear * (1.0 / 12.0))
    t12 = (b11 - 2.0 * m23 + 0.5 * q11) * (1.4 / 24.0)
    quarter = shear * 0.25
    t13 = (e1 - e2 - jx * uy) * quarter
    t14 = (e5 - e6 - jy * uz) * quarter
    t15 = (e3 - e4 - jx * uz) * quarter
    t16 = (gp - hp) * (1.98 / 8.0)
    t17 = (kp - gm) * (1.98 / 8.0)
    t18 = (hm - km) * (1.98 / 8.0)
    axis = -11.0 * t1 - 4.0 * t2
    edge = 8.0 * t1 + t2
    p9 = t9 - 2.0 * t10
    p11 = t11 - 2.0 * t12
    r9 = t9 + t10
    r11 = t11 + t12
    out = [None] * 19
    out[0] = f[0] + 30.0 * t1 - 12.0 * t2

    def put(i, even, odd):
        out[i] = f[i] - (even + odd)
        out[i + 1] = f[i + 1] - (even - odd)

    put(1, axis + 2.0 * p9, -4.0 * t4)
    put(3, axis - p9 + p11, -4.0 * t6)
    put(5, axis - p9 - p11, -4.0 * t8)
    vxy, vxz, vyz = edge + r9 + r11, edge + r9 - r11, edge - 2.0 * r9
    put(7, vxy + t13, t4 + t6 + (t16 - t17))
    put(9, vxy - t13, t4 - t6 + (t16 + t17))
    put(11, vxz + t15, t4 + t8 - (t16 - t18))
    put(13, vxz - t15, t4 - t8 - (t16 + t18))
    put(15, vyz + t14, t6 + t8 + (t17 - t18))
    put(17, vyz - t14, t6 - t8 + (t17 + t18))
    return out


def collide_kernel(par, pops, shear, post, near, far):
    even = par[0] == 0
    for plane in range(2):
        for half in range(2):
            rows = slice(8 * half, 8 * half + 8)
            rate = shear[plane, rows, :]
            out = relax([pops[i, plane, rows, :] for i in range(19)], rate)
            for i in range(19):
                post[i, plane, rows, :] = out[i]

    def own(field, plane):
        return shear[plane] if field == SHEAR else post[field, plane]

    for slot in range(20):
        up = own(X_LOW[slot][0], X_LOW[slot][1] + 2)
        down = own(X_HIGH[slot][0], X_HIGH[slot][1] - 2)
        near[slot] = jnp.where(even, up, down)
        far[slot] = jnp.where(even, down, up)


def reader(par, post, shear, near, far):
    even = par[0] == 0

    def main(q, rows=slice(0, 16)):
        if q < 20:
            return jnp.where(even, far[q, rows, :], near[q, rows, :])
        if q >= 60:
            return jnp.where(even, near[q - 60, rows, :], far[q - 60, rows, :])
        field, plane = PAIRS[q]
        return shear[plane, rows, :] if field == SHEAR else post[field, plane, rows, :]

    return main


def z_pack_kernel(par, post, shear, xnear, xfar, dep, near, far):
    main = reader(par, post, shear, xnear, xfar)
    even = par[2] == 0
    lane = lax.broadcasted_iota(jnp.int32, (16, 128), 1)
    for tile in range(2):
        high = jnp.zeros((16, 128), jnp.float32)
        low = jnp.zeros((16, 128), jnp.float32)
        for slot in range(FIRST if tile == 0 else len(PAIRS) - FIRST):
            value = main(tile * FIRST + slot)
            mine = (lane >= 3 * slot) & (lane < 3 * slot + 3)
            high = jnp.where(mine, pltpu.roll(value, (3 * slot + 3) % 128, 1), high)
            low = jnp.where(mine, pltpu.roll(value, 3 * slot, 1), low)
        if tile == 1:
            for field in range(4):
                for plane in range(2):
                    spot = DEP_LANE + 2 * field + plane
                    here = lane == spot
                    up = dep[field, 5, plane]
                    down = dep[field, 6, plane]
                    high = jnp.where(here, pltpu.roll(up, spot + 1, 1), high)
                    low = jnp.where(here, pltpu.roll(down, spot, 1), low)
        near[tile] = jnp.where(even, high, low)
        far[tile] = jnp.where(even, low, high)


def y_pack_kernel(par, post, shear, xnear, xfar, znear, zfar, dep, near, far):
    main = reader(par, post, shear, xnear, xfar)
    even = par[1] == 0
    even_z = par[2] == 0

    def put(row, count, high, low):
        near[row : row + count, :] = jnp.where(even, high, low)
        far[row : row + count, :] = jnp.where(even, low, high)

    top, bottom = slice(13, 16), slice(0, 3)
    for q in range(len(PAIRS)):
        put(3 * q, 3, main(q, top), main(q, bottom))
    for field in range(4):
        for plane in range(2):
            row = 240 + 2 * field + plane
            put(row, 1, dep[field, 3, plane, 15:16, :], dep[field, 4, plane, 0:1, :])
    for tile in range(2):
        put(
            248 + 3 * tile,
            3,
            jnp.where(even_z, zfar[tile, top, :], znear[tile, top, :]),
            jnp.where(even_z, zfar[tile, bottom, :], znear[tile, bottom, :]),
        )
        put(
            254 + 3 * tile,
            3,
            jnp.where(even_z, znear[tile, top, :], zfar[tile, top, :]),
            jnp.where(even_z, znear[tile, bottom, :], zfar[tile, bottom, :]),
        )
    near[260:264, :] = jnp.zeros((4, 128), jnp.float32)
    far[260:264, :] = jnp.zeros((4, 128), jnp.float32)


def shifted(value, shift_y, shift_z):
    if shift_y:
        value = pltpu.roll(value, shift_y % 24, 0)
    if shift_z:
        value = pltpu.roll(value, shift_z % 256, 1)
    return value


def step_kernel(
    par,
    post,
    shear,
    xnear,
    xfar,
    znear,
    zfar,
    ynear,
    yfar,
    dep,
    pops_out,
    fluid,
    partial,
    snear,
    sfar,
    columns,
    field_ext,
    second,
):
    main = reader(par, post, shear, xnear, xfar)
    even_x, even_y, even_z = par[0] == 0, par[1] == 0, par[2] == 0

    def y_low(row, count):
        return jnp.where(even_y, yfar[row : row + count, :], ynear[row : row + count, :])

    def y_high(row, count):
        return jnp.where(even_y, ynear[row : row + count, :], yfar[row : row + count, :])

    zero = jnp.zeros((8, 128), jnp.float32)
    for tile in range(2):
        for side in range(2):
            a, b = (zfar, znear) if side == 0 else (znear, zfar)
            columns[side, tile, 0:16, :] = jnp.where(even_z, a[tile], b[tile])
            columns[side, tile, 16:24, :] = zero
            row = 248 + 6 * side + 3 * tile
            columns[side, tile, 16:19, :] = y_high(row, 3)
            columns[side, tile, 21:24, :] = y_low(row, 3)
    lane = lax.broadcasted_iota(jnp.int32, (24, 128), 1)
    for q in range(len(PAIRS)):
        tile, slot = (0, q) if q < FIRST else (1, q - FIRST)
        field_ext[q, 0:16, 0:128] = main(q)
        field_ext[q, 16:24, 0:128] = zero
        field_ext[q, 16:19, 0:128] = y_high(3 * q, 3)
        field_ext[q, 21:24, 0:128] = y_low(3 * q, 3)
        low = pltpu.roll(columns[0, tile], (125 - 3 * slot) % 128, 1)
        high = pltpu.roll(columns[1, tile], (-3 * slot) % 128, 1)
        field_ext[q, :, 128:256] = jnp.where(lane < 64, high, low)

    for plane in range(4):
        for i in range(19):
            cx, cy, cz = SPEEDS[i]
            value = field_ext[INDEX[(i, plane - 1 - cx)]]
            second[i, plane] = shifted(value, cy, cz).reshape(3, 8, 256)

    for plane in range(4):
        rates = INDEX[(SHEAR, plane - 1)]

        def body(t, carry, plane=plane, rates=rates):
            row = pl.multiple_of(t * 8, 8)
            for z in range(2):
                lanes = slice(128 * z, 128 * z + 128)
                rate = field_ext[rates, pl.ds(row, 8), lanes]
                out = relax([second[i, plane, t, :, lanes] for i in range(19)], rate)
                for i in range(19):
                    second[i, plane, t, :, lanes] = out[i]
            return carry

        lax.fori_loop(0, 3, body, 0)

    lane16 = lax.broadcasted_iota(jnp.int32, (16, 128), 1)
    row8 = lax.broadcasted_iota(jnp.int32, (8, 128), 0)
    totals = [[None, None] for _ in range(4)]
    ups, downs = [None] * 4, [None] * 4
    for plane in range(2):
        rho = jx = jy = jz = None

        def add(total, value, sign):
            if sign == 0:
                return total
            if total is None:
                return value if sign > 0 else -value
            return total + value if sign > 0 else total - value

        for i in range(19):
            cx, cy, cz = SPEEDS[i]
            value = shifted(second[i, plane + 1 - cx].reshape(24, 256), cy, cz)
            pops_out[i, plane] = value[0:16, 0:128]
            rho = add(rho, value, 1)
            jx, jy, jz = add(jx, value, cx), add(jy, value, cy), add(jz, value, cz)
        u = [jx / rho, jy / rho, jz / rho]
        for c in range(3):
            fluid[c, plane] = u[c][0:16, 0:128]

        def moved(k, speed):
            s = dep[3, k, plane]
            return [dep[c, k, plane] - speed[c] * s for c in range(3)] + [2.0 * s]

        inner = [u[c][0:16, 0:128] for c in range(3)]
        total = moved(0, inner)
        tops = moved(1, inner)
        bottoms = moved(2, inner)

        def y_ext(k):
            ghosts = []
            for c in range(4):
                row = 240 + 2 * c + plane
                if k == 3:
                    ghost = jnp.where(row8 == 7, jnp.broadcast_to(y_low(row, 1), (8, 128)), 0.0)
                else:
                    ghost = jnp.where(row8 == 0, jnp.broadcast_to(y_high(row, 1), (8, 128)), 0.0)
                ghosts.append(jnp.concatenate([dep[c, k, plane], ghost], 0))
            return ghosts

        def z_ext(k):
            ghosts = []
            for c in range(4):
                spot = DEP_LANE + 2 * c + plane
                if k == 5:
                    ghost = pltpu.roll(columns[0, 1, 0:16, :], (127 - spot) % 128, 1)
                    ghost = jnp.where(lane16 == 127, ghost, 0.0)
                else:
                    ghost = pltpu.roll(columns[1, 1, 0:16, :], (-spot) % 128, 1)
                    ghost = jnp.where(lane16 == 0, ghost, 0.0)
                ghosts.append(jnp.concatenate([dep[c, k, plane], ghost], 1))
            return ghosts

        for k, shift in ((3, 1), (4, 23)):
            v = y_ext(k)
            rows = [v[c] - jnp.where(v[3] != 0.0, u[c][:, 0:128] * v[3], 0.0) for c in range(3)]
            rows.append(2.0 * v[3])
            for c in range(4):
                total[c] = total[c] + pltpu.roll(rows[c], shift, 0)[0:16, :]
        for k, shift in ((5, 1), (6, 255)):
            v = z_ext(k)
            rows = [v[c] - jnp.where(v[3] != 0.0, u[c][0:16, :] * v[3], 0.0) for c in range(3)]
            rows.append(2.0 * v[3])
            for c in range(4):
                total[c] = total[c] + pltpu.roll(rows[c], shift, 1)[:, 0:128]
        for c in range(4):
            totals[c][plane] = total[c]
        if plane == 0:
            downs, held = bottoms, tops
        else:
            ups = tops
            for c in range(4):
                totals[c][0] = totals[c][0] + bottoms[c]
                totals[c][1] = totals[c][1] + held[c]
    for c in range(4):
        partial[c, 0] = totals[c][0]
        partial[c, 1] = totals[c][1]
        snear[c] = jnp.where(even_x, ups[c], downs[c])
        sfar[c] = jnp.where(even_x, downs[c], ups[c])


def join_kernel(par, partial, near, far, out):
    even = par[0] == 0
    for c in range(4):
        out[c, 0] = partial[c, 0] + jnp.where(even, far[c], near[c])
        out[c, 1] = partial[c, 1] + jnp.where(even, near[c], far[c])


def deposit_kernel(cell, move, mask, mass, velocity, out, picked, keys):
    where = cell[...]
    code = (move[...] * 32 + jnp.right_shift(where, 7)).astype(jnp.float32).astype(jnp.bfloat16)
    spot = jnp.bitwise_and(where, 127).astype(jnp.float32).astype(jnp.bfloat16)
    weight = 0.5 * mask[...].astype(jnp.float32) * mass[...]
    rows = lax.broadcasted_iota(jnp.int32, (256, where.shape[1]), 0)
    rows = rows.astype(jnp.float32).astype(jnp.bfloat16)
    one, zero = jnp.bfloat16(1), jnp.bfloat16(0)
    keys[...] = jnp.where(rows == code, one, zero)
    here = rows[0:128] == spot
    for c in range(4):
        value = weight * velocity[c : c + 1, :] if c < 3 else weight
        coarse = value.astype(jnp.bfloat16)
        fine = (value - coarse.astype(jnp.float32)).astype(jnp.bfloat16)
        picked[256 * c : 256 * c + 128, :] = jnp.where(here, coarse, zero)
        picked[256 * c + 128 : 256 * c + 256, :] = jnp.where(here, fine, zero)
    total = lax.dot_general(
        keys[...], picked[...], (((1,), (1,)), ((), ())), preferred_element_type=jnp.float32
    )
    for c in range(4):
        out[c] = total[:, 256 * c : 256 * c + 128] + total[:, 256 * c + 128 : 256 * c + 256]


def drag_kernel(cell, mask, velocity, fluid, out):
    for group in range(8):
        rows = slice(8 * group, 8 * group + 8)
        where = cell[rows, :]
        lane = jnp.bitwise_and(where, 127)
        line = jnp.right_shift(where, 7)
        picked = [jnp.zeros((8, 128), jnp.float32) for _ in range(3)]
        for r in range(32):
            mine = line == r
            for c in range(3):
                table = jnp.broadcast_to(fluid[c, r : r + 1, :], (8, 128))
                value = jnp.take_along_axis(table, lane, axis=1)
                picked[c] = jnp.where(mine, value, picked[c])
        half = 0.5 * mask[rows, :].astype(jnp.float32)
        for c in range(3):
            old = velocity[c, rows, :]
            out[c, rows, :] = old + half * (picked[c] - old)


def swap(value, axis, shifted_by_one):
    count = lax.axis_size(axis)
    pairs = []
    for i in range(count):
        if shifted_by_one:
            pairs.append((i, (i + 1) % count if i % 2 else (i - 1) % count))
        else:
            pairs.append((i, i ^ 1))
    return lax.ppermute(value, axis, pairs)


def both_swaps(near, far, axis):
    return swap(near, axis, False), swap(far, axis, True)


def cost(flops, size):
    return pl.CostEstimate(flops=flops, bytes_accessed=size, transcendentals=0)


def struct(*shape):
    return jax.ShapeDtypeStruct(shape, jnp.float32)


def per_device(populations, shear_rate, part_cell, part_move, part_mask, part_velocity, part_mass):
    par = jnp.stack([lax.axis_index(a) % 2 for a in ("gx", "gy", "gz")]).astype(jnp.int32)
    count = part_cell.shape[0]
    limit = pltpu.CompilerParams(vmem_limit_bytes=40 << 20)

    post, near, far = pl.pallas_call(
        collide_kernel,
        out_shape=(struct(19, 2, 16, 128), struct(20, 16, 128), struct(20, 16, 128)),
        in_specs=[SMEM, VMEM, VMEM],
        out_specs=(VMEM,) * 3,
        compiler_params=limit,
        cost_estimate=cost(2000000, 2000000),
        name="collide",
    )(par, populations, shear_rate)
    xnear, xfar = both_swaps(near, far, "gx")

    flat = (1, count)
    dep = pl.pallas_call(
        deposit_kernel,
        out_shape=struct(4, 256, 128),
        in_specs=[VMEM] * 5,
        out_specs=VMEM,
        scratch_shapes=[
            pltpu.VMEM((1024, count), jnp.bfloat16),
            pltpu.VMEM((256, count), jnp.bfloat16),
        ],
        compiler_params=limit,
        cost_estimate=cost(4000000000, 1000000),
        name="deposit",
    )(
        part_cell.reshape(flat),
        part_move.reshape(flat),
        part_mask.reshape(flat),
        part_mass.reshape(flat),
        part_velocity,
    )
    dep = dep.reshape(4, 8, 2, 16, 128)

    near, far = pl.pallas_call(
        z_pack_kernel,
        out_shape=(struct(2, 16, 128), struct(2, 16, 128)),
        in_specs=[SMEM] + [VMEM] * 5,
        out_specs=(VMEM,) * 2,
        compiler_params=limit,
        cost_estimate=cost(500000, 1000000),
        name="z_pack",
    )(par, post, shear_rate, xnear, xfar, dep)
    znear, zfar = both_swaps(near, far, "gz")

    near, far = pl.pallas_call(
        y_pack_kernel,
        out_shape=(struct(Y_ROWS, 128), struct(Y_ROWS, 128)),
        in_specs=[SMEM] + [VMEM] * 7,
        out_specs=(VMEM,) * 2,
        compiler_params=limit,
        cost_estimate=cost(500000, 1000000),
        name="y_pack",
    )(par, post, shear_rate, xnear, xfar, znear, zfar, dep)
    ynear, yfar = both_swaps(near, far, "gy")

    populations_out, fluid, partial, near, far = pl.pallas_call(
        step_kernel,
        out_shape=(
            struct(19, 2, 16, 128),
            struct(3, 2, 16, 128),
            struct(4, 2, 16, 128),
            struct(4, 16, 128),
            struct(4, 16, 128),
        ),
        in_specs=[SMEM] + [VMEM] * 9,
        out_specs=(VMEM,) * 5,
        scratch_shapes=[
            pltpu.VMEM((2, 2, 24, 128), jnp.float32),
            pltpu.VMEM((len(PAIRS), 24, 256), jnp.float32),
            pltpu.VMEM((19, 4, 3, 8, 256), jnp.float32),
        ],
        compiler_params=limit,
        cost_estimate=cost(20000000, 4000000),
        name="step",
    )(par, post, shear_rate, xnear, xfar, znear, zfar, ynear, yfar, dep)
    snear, sfar = both_swaps(near, far, "gx")

    tall = (count // 128, 128)
    velocity_out = pl.pallas_call(
        drag_kernel,
        out_shape=struct(3, *tall),
        in_specs=[VMEM] * 4,
        out_specs=VMEM,
        compiler_params=limit,
        cost_estimate=cost(5000000, 1000000),
        name="drag",
    )(
        part_cell.reshape(tall),
        part_mask.reshape(tall),
        part_velocity.reshape(3, *tall),
        fluid.reshape(3, 32, 128),
    )
    velocity_out = velocity_out.reshape(3, count)

    sources = pl.pallas_call(
        join_kernel,
        out_shape=struct(4, 2, 16, 128),
        in_specs=[SMEM] + [VMEM] * 3,
        out_specs=VMEM,
        compiler_params=limit,
        cost_estimate=cost(100000, 300000),
        name="join",
    )(par, partial, snear, sfar)
    return populations_out, sources, velocity_out


def solution(mesh):
    placed = (
        P(None, "gx", "gy", "gz"),
        P("gx", "gy", "gz"),
        P(("gx", "gy", "gz")),
        P(("gx", "gy", "gz")),
        P(("gx", "gy", "gz")),
        P(None, ("gx", "gy", "gz")),
        P(("gx", "gy", "gz")),
    )
    return jax.shard_map(
        per_device,
        mesh=mesh,
        in_specs=placed,
        out_specs=(
            P(None, "gx", "gy", "gz"),
            P(None, "gx", "gy", "gz"),
            P(None, ("gx", "gy", "gz")),
        ),
        check_vma=False,
    )
```

```python
import functools

import jax
import jax.numpy as jnp
from jax import lax
from jax.experimental import pallas as pl
from jax.experimental.pallas import tpu as pltpu
from jax.sharding import PartitionSpec as P

SPEEDS = (
    (0, 0, 0),
    (1, 0, 0),
    (-1, 0, 0),
    (0, 1, 0),
    (0, -1, 0),
    (0, 0, 1),
    (0, 0, -1),
    (1, 1, 0),
    (-1, -1, 0),
    (1, -1, 0),
    (-1, 1, 0),
    (1, 0, 1),
    (-1, 0, -1),
    (1, 0, -1),
    (-1, 0, 1),
    (0, 1, 1),
    (0, -1, -1),
    (0, 1, -1),
    (0, -1, 1),
)
SHEAR = 19
UP = [i for i in range(19) if SPEEDS[i][0] == 1]
FLAT = [i for i in range(19) if SPEEDS[i][0] == 0]
DOWN = [i for i in range(19) if SPEEDS[i][0] == -1]
X_LOW = [(f, -1) for f in UP + FLAT + [SHEAR]] + [(f, -2) for f in UP]
X_HIGH = [(f, 2) for f in DOWN + FLAT + [SHEAR]] + [(f, 3) for f in DOWN]
PAIRS = X_LOW + [(f, 0) for f in range(20)] + [(f, 1) for f in range(20)] + X_HIGH
INDEX = {pair: q for q, pair in enumerate(PAIRS)}
DEP_LANE = 120
Y_ROWS = 272
X_ROWS = 152
TOP, BOTTOM = slice(13, 16), slice(0, 3)


def column_spot(field, plane):
    tile = 0 if plane < 0 else 2 if plane > 1 else 1
    return tile, 20 * (plane - 2 * (tile - 1)) + field


VMEM = pl.BlockSpec(memory_space=pltpu.VMEM)
SMEM = pl.BlockSpec(memory_space=pltpu.SMEM)
HBM = pl.BlockSpec(memory_space=pltpu.HBM)


def relax(f, shear):
    s1, s2, s3 = f[1] + f[2], f[3] + f[4], f[5] + f[6]
    d1, d2, d3 = f[1] - f[2], f[3] - f[4], f[5] - f[6]
    e1, e2, e3 = f[7] + f[8], f[9] + f[10], f[11] + f[12]
    e4, e5, e6 = f[13] + f[14], f[15] + f[16], f[17] + f[18]
    g1, g2, g3 = f[7] - f[8], f[9] - f[10], f[11] - f[12]
    g4, g5, g6 = f[13] - f[14], f[15] - f[16], f[17] - f[18]
    exy, exz, eyz = e1 + e2, e3 + e4, e5 + e6
    s23, m23 = s2 + s3, s2 - s3
    axes = s1 + s23
    exx = exy + exz
    edges = exx + eyz
    rho = f[0] + axes + edges
    gp, gm = g1 + g2, g1 - g2
    hp, hm = g3 + g4, g3 - g4
    kp, km = g5 + g6, g5 - g6
    gx, gy, gz = gp + hp, gm + kp, hm + km
    jx, jy, jz = d1 + gx, d2 + gy, d3 + gz
    inv = 1.0 / rho
    ux, uy, uz = jx * inv, jy * inv, jz * inv
    xx, yy, zz = jx * ux, jy * uy, jz * uz
    sq = xx + yy + zz
    n1 = 8.0 * edges - 11.0 * axes - 30.0 * f[0] + (11.0 * rho - 19.0 * sq)
    n2 = 12.0 * f[0] - 4.0 * axes + edges - (3.0 * rho - 5.5 * sq)
    a9 = 2.0 * s1 - s23
    b9 = exx - 2.0 * eyz
    q9 = 3.0 * xx - sq
    b11 = exy - exz
    q11 = yy - zz
    t1 = n1 * (1.19 / 2394.0)
    t2 = n2 * (1.4 / 252.0)
    t4 = (gx - 4.0 * d1 + (2.0 / 3.0) * jx) * (1.2 / 40.0)
    t6 = (gy - 4.0 * d2 + (2.0 / 3.0) * jy) * (1.2 / 40.0)
    t8 = (gz - 4.0 * d3 + (2.0 / 3.0) * jz) * (1.2 / 40.0)
    t9 = (a9 + b9 - q9) * (shear * (1.0 / 36.0))
    t10 = (b9 - 2.0 * a9 + 0.5 * q9) * (1.4 / 72.0)
    t11 = (m23 + b11 - q11) * (shear * (1.0 / 12.0))
    t12 = (b11 - 2.0 * m23 + 0.5 * q11) * (1.4 / 24.0)
    quarter = shear * 0.25
    t13 = (e1 - e2 - jx * uy) * quarter
    t14 = (e5 - e6 - jy * uz) * quarter
    t15 = (e3 - e4 - jx * uz) * quarter
    t16 = (gp - hp) * (1.98 / 8.0)
    t17 = (kp - gm) * (1.98 / 8.0)
    t18 = (hm - km) * (1.98 / 8.0)
    axis = -11.0 * t1 - 4.0 * t2
    edge = 8.0 * t1 + t2
    p9 = t9 - 2.0 * t10
    p11 = t11 - 2.0 * t12
    r9 = t9 + t10
    r11 = t11 + t12
    out = [None] * 19
    out[0] = f[0] + 30.0 * t1 - 12.0 * t2

    def put(i, even, odd):
        out[i] = f[i] - (even + odd)
        out[i + 1] = f[i + 1] - (even - odd)

    put(1, axis + 2.0 * p9, -4.0 * t4)
    put(3, axis - p9 + p11, -4.0 * t6)
    put(5, axis - p9 - p11, -4.0 * t8)
    vxy, vxz, vyz = edge + r9 + r11, edge + r9 - r11, edge - 2.0 * r9
    put(7, vxy + t13, t4 + t6 + (t16 - t17))
    put(9, vxy - t13, t4 - t6 + (t16 + t17))
    put(11, vxz + t15, t4 + t8 - (t16 - t18))
    put(13, vxz - t15, t4 - t8 - (t16 + t18))
    put(15, vyz + t14, t6 + t8 + (t17 - t18))
    put(17, vyz - t14, t6 - t8 + (t17 + t18))
    return out


def collide_kernel(par, pops_hbm, shear_hbm, post, bulk_near, bulk_far, near, far, pops, sems):
    even = par[0] == 0
    rate_copy = pltpu.make_async_copy(shear_hbm, post.at[SHEAR], sems.at[4])
    rate_copy.start()
    copies = []
    for plane in range(2):
        for half in range(2):
            rows = slice(8 * half, 8 * half + 8)
            copy = pltpu.make_async_copy(
                pops_hbm.at[:, plane, rows, :], pops.at[:, plane, rows, :], sems.at[2 * plane + half]
            )
            copy.start()
            copies.append(copy)
    rate_copy.wait()
    for plane in range(2):
        for half in range(2):
            rows = slice(8 * half, 8 * half + 8)
            copies[2 * plane + half].wait()
            rate = post[SHEAR, plane, rows, :]
            out = relax([pops[i, plane, rows, :] for i in range(19)], rate)
            for i in range(19):
                post[i, plane, rows, :] = out[i]

    lane = lax.broadcasted_iota(jnp.int32, (16, 128), 1)
    high = jnp.zeros((16, 128), jnp.float32)
    low = jnp.zeros((16, 128), jnp.float32)
    for plane in range(2):
        for field in range(20):
            value, slot = post[field, plane], 20 * plane + field
            mine = (lane >= 3 * slot) & (lane < 3 * slot + 3)
            high = jnp.where(mine, pltpu.roll(value, (3 * slot + 3) % 128, 1), high)
            low = jnp.where(mine, pltpu.roll(value, 3 * slot, 1), low)
    for message in (near, far):
        message[0:16, :] = high
        message[16:32, :] = low
    for slot in range(20):
        up = post[X_LOW[slot][0], X_LOW[slot][1] + 2]
        down = post[X_HIGH[slot][0], X_HIGH[slot][1] - 2]
        one = jnp.where(even, up, down)
        two = jnp.where(even, down, up)
        bulk_near[slot] = one
        bulk_far[slot] = two
        for n, rows in enumerate((BOTTOM, TOP)):
            at = 32 + 6 * slot + 3 * n
            near[at : at + 3, :] = one[rows, :]
            far[at : at + 3, :] = two[rows, :]


def reader(par, post, near, far):
    even = par[0] == 0

    def main(q, rows=slice(0, 16)):
        if q < 20:
            return jnp.where(even, far[q, rows, :], near[q, rows, :])
        if q >= 60:
            return jnp.where(even, near[q - 60, rows, :], far[q - 60, rows, :])
        field, plane = PAIRS[q]
        return post[field, plane, rows, :]

    return main


def z_pack_kernel(par, own, xnear, xfar, edge, near, far):
    faces = (slice(0, 16), slice(16, 32))
    even_x, even_z = par[0] == 0, par[2] == 0
    lane = lax.broadcasted_iota(jnp.int32, (16, 128), 1)
    sums = edge[...] + pltpu.roll(edge[...], 112, 1)
    sides = []
    for n, face in enumerate(faces):
        placed = pltpu.roll(sums, DEP_LANE - 8 * n, 1)
        placed = jnp.where(jnp.bitwise_and(lane, 1) == 1, placed[16:32, :], placed[0:16, :])
        sides.append(
            (
                jnp.where(even_x, xfar[face, :], xnear[face, :]),
                jnp.where(lane >= DEP_LANE, placed, own[face, :]),
                jnp.where(even_x, xnear[face, :], xfar[face, :]),
            )
        )
    for tile in range(3):
        near[tile] = jnp.where(even_z, sides[0][tile], sides[1][tile])
        far[tile] = jnp.where(even_z, sides[1][tile], sides[0][tile])


def y_pack_kernel(par, post, xnear, xfar, znear, zfar, edge, near, far):
    even_x, even, even_z = par[0] == 0, par[1] == 0, par[2] == 0

    def main(q, rows):
        at = 32 + 6 * (q % 20) + (0 if rows == BOTTOM else 3)
        if q < 20:
            return jnp.where(even_x, xfar[at : at + 3, :], xnear[at : at + 3, :])
        if q >= 60:
            return jnp.where(even_x, xnear[at : at + 3, :], xfar[at : at + 3, :])
        return post[PAIRS[q][0], PAIRS[q][1], rows, :]

    def put(row, count, high, low):
        near[row : row + count, :] = jnp.where(even, high, low)
        far[row : row + count, :] = jnp.where(even, low, high)

    for q in range(len(PAIRS)):
        put(3 * q, 3, main(q, TOP), main(q, BOTTOM))
    put(240, 8, edge[0:8, :], edge[8:16, :])
    for tile in range(3):
        put(
            248 + 3 * tile,
            3,
            jnp.where(even_z, zfar[tile, TOP, :], znear[tile, TOP, :]),
            jnp.where(even_z, zfar[tile, BOTTOM, :], znear[tile, BOTTOM, :]),
        )
        put(
            257 + 3 * tile,
            3,
            jnp.where(even_z, znear[tile, TOP, :], zfar[tile, TOP, :]),
            jnp.where(even_z, znear[tile, BOTTOM, :], zfar[tile, BOTTOM, :]),
        )
    near[266:272, :] = jnp.zeros((6, 128), jnp.float32)
    far[266:272, :] = jnp.zeros((6, 128), jnp.float32)


def shifted(value, shift_y, shift_z):
    if shift_y:
        value = pltpu.roll(value, shift_y % 24, 0)
    if shift_z:
        value = pltpu.roll(value, shift_z % 256, 1)
    return value


def step_kernel(
    par,
    post,
    xnear,
    xfar,
    znear,
    zfar,
    ynear,
    yfar,
    dep_a,
    dep_b,
    pops_out,
    fluid,
    partial,
    snear,
    sfar,
    columns,
    field_ext,
    second,
):
    main = reader(par, post, xnear, xfar)
    even_x, even_y, even_z = par[0] == 0, par[1] == 0, par[2] == 0

    def dep(c, k, plane):
        return (dep_a if c < 2 else dep_b)[c % 2, k, plane]

    def y_low(row, count):
        return jnp.where(even_y, yfar[row : row + count, :], ynear[row : row + count, :])

    def y_high(row, count):
        return jnp.where(even_y, ynear[row : row + count, :], yfar[row : row + count, :])

    zero = jnp.zeros((8, 128), jnp.float32)
    for tile in range(3):
        for side in range(2):
            a, b = (zfar, znear) if side == 0 else (znear, zfar)
            columns[side, tile, 0:16, :] = jnp.where(even_z, a[tile], b[tile])
            columns[side, tile, 16:24, :] = zero
            row = 248 + 9 * side + 3 * tile
            columns[side, tile, 16:19, :] = y_high(row, 3)
            columns[side, tile, 21:24, :] = y_low(row, 3)
    lane = lax.broadcasted_iota(jnp.int32, (24, 128), 1)
    for q in range(len(PAIRS)):
        tile, slot = column_spot(*PAIRS[q])
        field_ext[q, 0:16, 0:128] = main(q)
        field_ext[q, 16:24, 0:128] = zero
        field_ext[q, 16:19, 0:128] = y_high(3 * q, 3)
        field_ext[q, 21:24, 0:128] = y_low(3 * q, 3)
        low = pltpu.roll(columns[0, tile], (125 - 3 * slot) % 128, 1)
        high = pltpu.roll(columns[1, tile], (-3 * slot) % 128, 1)
        field_ext[q, :, 128:256] = jnp.where(lane < 64, high, low)

    for plane in range(4):
        for i in range(19):
            cx, cy, cz = SPEEDS[i]
            value = field_ext[INDEX[(i, plane - 1 - cx)]]
            second[i, plane] = shifted(value, cy, cz).reshape(3, 8, 256)

    for plane in range(4):
        rates = INDEX[(SHEAR, plane - 1)]

        def body(t, carry, plane=plane, rates=rates):
            row = pl.multiple_of(t * 8, 8)
            for z in range(2):
                lanes = slice(128 * z, 128 * z + 128)
                rate = field_ext[rates, pl.ds(row, 8), lanes]
                out = relax([second[i, plane, t, :, lanes] for i in range(19)], rate)
                for i in range(19):
                    second[i, plane, t, :, lanes] = out[i]
            return carry

        lax.fori_loop(0, 3, body, 0)

    lane16 = lax.broadcasted_iota(jnp.int32, (16, 128), 1)
    row8 = lax.broadcasted_iota(jnp.int32, (8, 128), 0)
    totals = [[None, None] for _ in range(4)]
    ups, downs = [None] * 4, [None] * 4
    for plane in range(2):
        rho = jx = jy = jz = None

        def add(total, value, sign):
            if sign == 0:
                return total
            if total is None:
                return value if sign > 0 else -value
            return total + value if sign > 0 else total - value

        for i in range(19):
            cx, cy, cz = SPEEDS[i]
            value = shifted(second[i, plane + 1 - cx].reshape(24, 256), cy, cz)
            pops_out[i, plane] = value[0:16, 0:128]
            rho = add(rho, value, 1)
            jx, jy, jz = add(jx, value, cx), add(jy, value, cy), add(jz, value, cz)
        u = [jx / rho, jy / rho, jz / rho]
        for c in range(3):
            fluid[c, plane] = u[c][0:16, 0:128]

        def moved(k, speed):
            s = dep(3, k, plane)
            return [dep(c, k, plane) - speed[c] * s for c in range(3)] + [2.0 * s]

        inner = [u[c][0:16, 0:128] for c in range(3)]
        total = moved(0, inner)
        tops = moved(1, inner)
        bottoms = moved(2, inner)

        def y_ext(k):
            ghosts = []
            for c in range(4):
                row = 240 + 2 * c + plane
                if k == 3:
                    ghost = jnp.where(row8 == 7, jnp.broadcast_to(y_low(row, 1), (8, 128)), 0.0)
                else:
                    ghost = jnp.where(row8 == 0, jnp.broadcast_to(y_high(row, 1), (8, 128)), 0.0)
                ghosts.append(jnp.concatenate([dep(c, k, plane), ghost], 0))
            return ghosts

        def z_ext(k):
            ghosts = []
            for c in range(4):
                spot = DEP_LANE + 2 * c + plane
                if k == 5:
                    ghost = pltpu.roll(columns[0, 1, 0:16, :], (127 - spot) % 128, 1)
                    ghost = jnp.where(lane16 == 127, ghost, 0.0)
                else:
                    ghost = pltpu.roll(columns[1, 1, 0:16, :], (-spot) % 128, 1)
                    ghost = jnp.where(lane16 == 0, ghost, 0.0)
                ghosts.append(jnp.concatenate([dep(c, k, plane), ghost], 1))
            return ghosts

        for k, shift in ((3, 1), (4, 23)):
            v = y_ext(k)
            rows = [v[c] - jnp.where(v[3] != 0.0, u[c][:, 0:128] * v[3], 0.0) for c in range(3)]
            rows.append(2.0 * v[3])
            for c in range(4):
                total[c] = total[c] + pltpu.roll(rows[c], shift, 0)[0:16, :]
        for k, shift in ((5, 1), (6, 255)):
            v = z_ext(k)
            rows = [v[c] - jnp.where(v[3] != 0.0, u[c][0:16, :] * v[3], 0.0) for c in range(3)]
            rows.append(2.0 * v[3])
            for c in range(4):
                total[c] = total[c] + pltpu.roll(rows[c], shift, 1)[:, 0:128]
        for c in range(4):
            totals[c][plane] = total[c]
        if plane == 0:
            downs, held = bottoms, tops
        else:
            ups = tops
            for c in range(4):
                totals[c][0] = totals[c][0] + bottoms[c]
                totals[c][1] = totals[c][1] + held[c]
    for c in range(4):
        partial[c, 0] = totals[c][0]
        partial[c, 1] = totals[c][1]
        snear[c] = jnp.where(even_x, ups[c], downs[c])
        sfar[c] = jnp.where(even_x, downs[c], ups[c])


def pieces(value):
    coarse = value.astype(jnp.bfloat16)
    return coarse, (value - coarse.astype(jnp.float32)).astype(jnp.bfloat16)


def small(value):
    return value.astype(jnp.float32).astype(jnp.bfloat16)


def numbers(rows, width):
    return lax.broadcasted_iota(jnp.int32, (rows, width), 0)


BY_LANE = (((1,), (1,)), ((), ()))


def deposit_kernel(fields, cell, move, mask, mass, velocity, out, picked, keys):
    where = cell[...]
    width = where.shape[1]
    code = small(move[...] * 32 + jnp.right_shift(where, 7))
    spot = small(jnp.bitwise_and(where, 127))
    weight = 0.5 * mask[...].astype(jnp.float32) * mass[...]
    rows = small(numbers(256, width))
    keys[...] = jnp.where(rows == code, jnp.bfloat16(1), jnp.bfloat16(0))
    here = rows[0:128] == spot
    for n, c in enumerate(fields):
        value = weight * velocity[c : c + 1, :] if c < 3 else weight
        for piece, part in enumerate(pieces(value)):
            at = 256 * n + 128 * piece
            picked[at : at + 128, :] = jnp.where(here, part, jnp.bfloat16(0))
    total = lax.dot_general(
        keys[...], picked[...], BY_LANE, preferred_element_type=jnp.float32
    )
    for n in range(2):
        out[n] = total[:, 256 * n : 256 * n + 128] + total[:, 256 * n + 128 : 256 * n + 256]


def edge_rows(mask, mass, velocity, target, code):
    weight = 0.5 * mask[...].astype(jnp.float32) * mass[...]
    width = weight.shape[1]
    values = [weight * velocity[c : c + 1, :] for c in range(3)] + [weight]
    field = jnp.bitwise_and(jnp.right_shift(numbers(16, width), 1), 3)
    chosen = jnp.where(field == 0, values[0], values[1])
    chosen = jnp.where(field == 2, values[2], chosen)
    chosen = jnp.where(field == 3, values[3], chosen)
    chosen = jnp.where(code == target, chosen, 0.0)
    return jnp.concatenate(pieces(chosen), 0)


def z_edge_kernel(cell, move, mask, mass, velocity, out):
    where = cell[...]
    width = where.shape[1]
    low = jnp.right_shift(numbers(16, width), 3)
    target = jnp.where(low == 0, 5 * 128 + 127, 6 * 128)
    code = move[...] * 128 + jnp.bitwise_and(where, 127)
    rows = edge_rows(mask, mass, velocity, target, code)
    line = jnp.where(
        small(numbers(32, width)) == small(jnp.right_shift(where, 7)), jnp.bfloat16(1), jnp.bfloat16(0)
    )
    out[...] = jnp.zeros_like(out)
    out[:, 0:32] = lax.dot_general(line, rows, BY_LANE, preferred_element_type=jnp.float32)


def y_edge_kernel(cell, move, mask, mass, velocity, out, tall):
    where = cell[...]
    width = where.shape[1]
    row = numbers(16, width)
    plane = jnp.bitwise_and(row, 1) * 16
    target = jnp.where(row < 8, 3 * 32 + 15 + plane, 4 * 32 + plane)
    code = move[...] * 32 + jnp.right_shift(where, 7)
    rows = edge_rows(mask, mass, velocity, target, code)
    here = jnp.where(
        small(numbers(128, width)) == small(jnp.bitwise_and(where, 127)), jnp.bfloat16(1), jnp.bfloat16(0)
    )
    total = lax.dot_general(rows, here, BY_LANE, preferred_element_type=jnp.float32)
    out[...] = total[0:16, :] + total[16:32, :]
    for j in range(width // 128):
        for c in range(3):
            tall[c, j : j + 1, :] = velocity[c : c + 1, 128 * j : 128 * j + 128]


def drag_kernel(cell, mask, velocity, fluid, out):
    for group in range(8):
        rows = slice(8 * group, 8 * group + 8)
        where = cell[rows, :]
        lane = jnp.bitwise_and(where, 127)
        line = jnp.right_shift(where, 7)
        picked = [jnp.zeros((8, 128), jnp.float32) for _ in range(3)]
        for r in range(32):
            mine = line == r
            for c in range(3):
                table = jnp.broadcast_to(fluid[c, r : r + 1, :], (8, 128))
                value = jnp.take_along_axis(table, lane, axis=1)
                picked[c] = jnp.where(mine, value, picked[c])
        half = 0.5 * mask[rows, :].astype(jnp.float32)
        for c in range(3):
            old = velocity[c, rows, :]
            new = old + half * (picked[c] - old)
            for r in range(8):
                at = 128 * (8 * group + r)
                out[c : c + 1, at : at + 128] = new[r : r + 1, :]


def swap(value, axis, shifted_by_one):
    count = lax.axis_size(axis)
    pairs = []
    for i in range(count):
        if shifted_by_one:
            pairs.append((i, (i + 1) % count if i % 2 else (i - 1) % count))
        else:
            pairs.append((i, i ^ 1))
    return lax.ppermute(value, axis, pairs)


def both_swaps(near, far, axis):
    far = swap(far, axis, True)
    near = swap(near, axis, False)
    return near, far


def struct(*shape):
    return jax.ShapeDtypeStruct(shape, jnp.float32)


def call(kernel, outs, args, specs=None, scratch=(), flops=1000000, size=1000000):
    single = not isinstance(outs, tuple)
    return pl.pallas_call(
        kernel,
        out_shape=outs,
        in_specs=specs or [VMEM] * len(args),
        out_specs=VMEM if single else (VMEM,) * len(outs),
        scratch_shapes=scratch,
        compiler_params=pltpu.CompilerParams(vmem_limit_bytes=40 << 20),
        cost_estimate=pl.CostEstimate(flops=flops, bytes_accessed=size, transcendentals=0),
    )(*args)


def body(populations, shear_rate, part_cell, part_move, part_mask, part_velocity, part_mass):
    par = jnp.stack([lax.axis_index(a) % 2 for a in ("gx", "gy", "gz")]).astype(jnp.int32)
    count = part_cell.shape[0]
    flat = (1, count)
    particles = (
        part_cell.reshape(flat),
        part_move.reshape(flat),
        part_mask.reshape(flat),
        part_mass.reshape(flat),
        part_velocity,
    )

    post, bulk_near, bulk_far, near, far = call(
        collide_kernel,
        (
            struct(20, 2, 16, 128),
            struct(20, 16, 128),
            struct(20, 16, 128),
            struct(X_ROWS, 128),
            struct(X_ROWS, 128),
        ),
        (
            par,
            pltpu.with_memory_space_constraint(populations, pltpu.HBM),
            pltpu.with_memory_space_constraint(shear_rate, pltpu.HBM),
        ),
        [SMEM, HBM, HBM],
        [pltpu.VMEM((19, 2, 16, 128), jnp.float32), pltpu.SemaphoreType.DMA((5,))],
    )
    xnear, xfar = both_swaps(near, far, "gx")
    own_columns = near

    edge = call(z_edge_kernel, struct(32, 128), particles)
    near, far = call(
        z_pack_kernel,
        (struct(3, 16, 128), struct(3, 16, 128)),
        (par, own_columns, xnear, xfar, edge),
        [SMEM] + [VMEM] * 4,
    )
    znear, zfar = both_swaps(near, far, "gz")
    bnear, bfar = both_swaps(bulk_near, bulk_far, "gx")

    edge, velocity_tall = call(
        y_edge_kernel, (struct(16, 128), struct(3, count // 128, 128)), particles
    )
    scratch = [pltpu.VMEM((512, count), jnp.bfloat16), pltpu.VMEM((256, count), jnp.bfloat16)]
    deposits = [
        call(
            functools.partial(deposit_kernel, fields),
            struct(2, 256, 128),
            particles,
            scratch=scratch,
            flops=2000000000,
        ).reshape(2, 8, 2, 16, 128)
        for fields in ((0, 1), (2, 3))
    ]
    near, far = call(
        y_pack_kernel,
        (struct(Y_ROWS, 128), struct(Y_ROWS, 128)),
        (par, post, xnear, xfar, znear, zfar, edge),
        [SMEM] + [VMEM] * 6,
    )
    ynear, yfar = both_swaps(near, far, "gy")

    populations_out, fluid, partial, near, far = call(
        step_kernel,
        (
            struct(19, 2, 16, 128),
            struct(3, 2, 16, 128),
            struct(4, 2, 16, 128),
            struct(4, 16, 128),
            struct(4, 16, 128),
        ),
        (par, post, bnear, bfar, znear, zfar, ynear, yfar, *deposits),
        [SMEM] + [VMEM] * 9,
        [
            pltpu.VMEM((2, 3, 24, 128), jnp.float32),
            pltpu.VMEM((len(PAIRS), 24, 256), jnp.float32),
            pltpu.VMEM((19, 4, 3, 8, 256), jnp.float32),
        ],
        flops=20000000,
    )
    snear, sfar = both_swaps(near, far, "gx")

    tall = (count // 128, 128)
    velocity_out = call(
        drag_kernel,
        struct(3, count),
        (
            part_cell.reshape(tall),
            part_mask.reshape(tall),
            velocity_tall,
            fluid.reshape(3, 32, 128),
        ),
    )

    even = par[0] == 0
    upper = lax.broadcasted_iota(jnp.int32, partial.shape, 1) == 1
    sources = partial + jnp.where(upper == even, snear[:, None], sfar[:, None])
    return populations_out, sources, velocity_out


def solution(mesh):
    placed = (
        P(None, "gx", "gy", "gz"),
        P("gx", "gy", "gz"),
        P(("gx", "gy", "gz")),
        P(("gx", "gy", "gz")),
        P(("gx", "gy", "gz")),
        P(None, ("gx", "gy", "gz")),
        P(("gx", "gy", "gz")),
    )
    return jax.shard_map(
        body,
        mesh=mesh,
        in_specs=placed,
        out_specs=(
            P(None, "gx", "gy", "gz"),
            P(None, "gx", "gy", "gz"),
            P(None, ("gx", "gy", "gz")),
        ),
        check_vma=False,
    )
```

```python
import functools

import jax
import jax.numpy as jnp
from jax import lax
from jax.experimental import pallas as pl
from jax.experimental.pallas import tpu as pltpu
from jax.sharding import PartitionSpec as P

SPEEDS = (
    (0, 0, 0),
    (1, 0, 0),
    (-1, 0, 0),
    (0, 1, 0),
    (0, -1, 0),
    (0, 0, 1),
    (0, 0, -1),
    (1, 1, 0),
    (-1, -1, 0),
    (1, -1, 0),
    (-1, 1, 0),
    (1, 0, 1),
    (-1, 0, -1),
    (1, 0, -1),
    (-1, 0, 1),
    (0, 1, 1),
    (0, -1, -1),
    (0, 1, -1),
    (0, -1, 1),
)
SHEAR = 19
UP = [i for i in range(19) if SPEEDS[i][0] == 1]
FLAT = [i for i in range(19) if SPEEDS[i][0] == 0]
DOWN = [i for i in range(19) if SPEEDS[i][0] == -1]
X_LOW = [(f, -1) for f in UP + FLAT + [SHEAR]] + [(f, -2) for f in UP]
X_HIGH = [(f, 2) for f in DOWN + FLAT + [SHEAR]] + [(f, 3) for f in DOWN]
PAIRS = X_LOW + [(f, 0) for f in range(20)] + [(f, 1) for f in range(20)] + X_HIGH
INDEX = {pair: q for q, pair in enumerate(PAIRS)}
FIRST = 42
DEP_LANE = 3 * (len(PAIRS) - FIRST)
Y_ROWS = 264
VMEM = pl.BlockSpec(memory_space=pltpu.VMEM)
SMEM = pl.BlockSpec(memory_space=pltpu.SMEM)
HBM = pl.BlockSpec(memory_space=pltpu.HBM)


def relax(f, shear):
    s1, s2, s3 = f[1] + f[2], f[3] + f[4], f[5] + f[6]
    d1, d2, d3 = f[1] - f[2], f[3] - f[4], f[5] - f[6]
    e1, e2, e3 = f[7] + f[8], f[9] + f[10], f[11] + f[12]
    e4, e5, e6 = f[13] + f[14], f[15] + f[16], f[17] + f[18]
    g1, g2, g3 = f[7] - f[8], f[9] - f[10], f[11] - f[12]
    g4, g5, g6 = f[13] - f[14], f[15] - f[16], f[17] - f[18]
    exy, exz, eyz = e1 + e2, e3 + e4, e5 + e6
    s23, m23 = s2 + s3, s2 - s3
    axes = s1 + s23
    exx = exy + exz
    edges = exx + eyz
    rho = f[0] + axes + edges
    gp, gm = g1 + g2, g1 - g2
    hp, hm = g3 + g4, g3 - g4
    kp, km = g5 + g6, g5 - g6
    gx, gy, gz = gp + hp, gm + kp, hm + km
    jx, jy, jz = d1 + gx, d2 + gy, d3 + gz
    inv = 1.0 / rho
    ux, uy, uz = jx * inv, jy * inv, jz * inv
    xx, yy, zz = jx * ux, jy * uy, jz * uz
    sq = xx + yy + zz
    n1 = 8.0 * edges - 11.0 * axes - 30.0 * f[0] + (11.0 * rho - 19.0 * sq)
    n2 = 12.0 * f[0] - 4.0 * axes + edges - (3.0 * rho - 5.5 * sq)
    a9 = 2.0 * s1 - s23
    b9 = exx - 2.0 * eyz
    q9 = 3.0 * xx - sq
    b11 = exy - exz
    q11 = yy - zz
    t1 = n1 * (1.19 / 2394.0)
    t2 = n2 * (1.4 / 252.0)
    t4 = (gx - 4.0 * d1 + (2.0 / 3.0) * jx) * (1.2 / 40.0)
    t6 = (gy - 4.0 * d2 + (2.0 / 3.0) * jy) * (1.2 / 40.0)
    t8 = (gz - 4.0 * d3 + (2.0 / 3.0) * jz) * (1.2 / 40.0)
    t9 = (a9 + b9 - q9) * (shear * (1.0 / 36.0))
    t10 = (b9 - 2.0 * a9 + 0.5 * q9) * (1.4 / 72.0)
    t11 = (m23 + b11 - q11) * (shear * (1.0 / 12.0))
    t12 = (b11 - 2.0 * m23 + 0.5 * q11) * (1.4 / 24.0)
    quarter = shear * 0.25
    t13 = (e1 - e2 - jx * uy) * quarter
    t14 = (e5 - e6 - jy * uz) * quarter
    t15 = (e3 - e4 - jx * uz) * quarter
    t16 = (gp - hp) * (1.98 / 8.0)
    t17 = (kp - gm) * (1.98 / 8.0)
    t18 = (hm - km) * (1.98 / 8.0)
    axis = -11.0 * t1 - 4.0 * t2
    edge = 8.0 * t1 + t2
    p9 = t9 - 2.0 * t10
    p11 = t11 - 2.0 * t12
    r9 = t9 + t10
    r11 = t11 + t12
    out = [None] * 19
    out[0] = f[0] + 30.0 * t1 - 12.0 * t2

    def put(i, even, odd):
        out[i] = f[i] - (even + odd)
        out[i + 1] = f[i + 1] - (even - odd)

    put(1, axis + 2.0 * p9, -4.0 * t4)
    put(3, axis - p9 + p11, -4.0 * t6)
    put(5, axis - p9 - p11, -4.0 * t8)
    vxy, vxz, vyz = edge + r9 + r11, edge + r9 - r11, edge - 2.0 * r9
    put(7, vxy + t13, t4 + t6 + (t16 - t17))
    put(9, vxy - t13, t4 - t6 + (t16 + t17))
    put(11, vxz + t15, t4 + t8 - (t16 - t18))
    put(13, vxz - t15, t4 - t8 - (t16 + t18))
    put(15, vyz + t14, t6 + t8 + (t17 - t18))
    put(17, vyz - t14, t6 - t8 + (t17 + t18))
    return out


def collide_kernel(par, pops_hbm, shear_hbm, post, near, far, pops, sems):
    even = par[0] == 0
    rate_copy = pltpu.make_async_copy(shear_hbm, post.at[SHEAR], sems.at[4])
    rate_copy.start()
    copies = []
    for plane in range(2):
        for half in range(2):
            rows = slice(8 * half, 8 * half + 8)
            copy = pltpu.make_async_copy(
                pops_hbm.at[:, plane, rows, :], pops.at[:, plane, rows, :], sems.at[2 * plane + half]
            )
            copy.start()
            copies.append(copy)
    rate_copy.wait()
    for plane in range(2):
        for half in range(2):
            rows = slice(8 * half, 8 * half + 8)
            copies[2 * plane + half].wait()
            rate = post[SHEAR, plane, rows, :]
            out = relax([pops[i, plane, rows, :] for i in range(19)], rate)
            for i in range(19):
                post[i, plane, rows, :] = out[i]

    for slot in range(20):
        up = post[X_LOW[slot][0], X_LOW[slot][1] + 2]
        down = post[X_HIGH[slot][0], X_HIGH[slot][1] - 2]
        near[slot] = jnp.where(even, up, down)
        far[slot] = jnp.where(even, down, up)


def reader(par, post, near, far):
    even = par[0] == 0

    def main(q, rows=slice(0, 16)):
        if q < 20:
            return jnp.where(even, far[q, rows, :], near[q, rows, :])
        if q >= 60:
            return jnp.where(even, near[q - 60, rows, :], far[q - 60, rows, :])
        field, plane = PAIRS[q]
        return post[field, plane, rows, :]

    return main


def z_pack_kernel(par, post, xnear, xfar, edge, near, far):
    main = reader(par, post, xnear, xfar)
    even = par[2] == 0
    lane = lax.broadcasted_iota(jnp.int32, (16, 128), 1)
    for tile in range(2):
        high = jnp.zeros((16, 128), jnp.float32)
        low = jnp.zeros((16, 128), jnp.float32)
        for slot in range(FIRST if tile == 0 else len(PAIRS) - FIRST):
            value = main(tile * FIRST + slot)
            mine = (lane >= 3 * slot) & (lane < 3 * slot + 3)
            high = jnp.where(mine, pltpu.roll(value, (3 * slot + 3) % 128, 1), high)
            low = jnp.where(mine, pltpu.roll(value, 3 * slot, 1), low)
        if tile == 1:
            sums = edge[...] + pltpu.roll(edge[...], 112, 1)
            odd = jnp.bitwise_and(lane - DEP_LANE, 1) == 1
            ours = (lane >= DEP_LANE) & (lane < DEP_LANE + 8)
            for shift in (DEP_LANE, DEP_LANE - 8):
                placed = pltpu.roll(sums, shift, 1)
                placed = jnp.where(odd, placed[16:32, :], placed[0:16, :])
                if shift == DEP_LANE:
                    high = jnp.where(ours, placed, high)
                else:
                    low = jnp.where(ours, placed, low)
        near[tile] = jnp.where(even, high, low)
        far[tile] = jnp.where(even, low, high)


def y_pack_kernel(par, post, xnear, xfar, znear, zfar, edge, near, far):
    main = reader(par, post, xnear, xfar)
    even = par[1] == 0
    even_z = par[2] == 0

    def put(row, count, high, low):
        near[row : row + count, :] = jnp.where(even, high, low)
        far[row : row + count, :] = jnp.where(even, low, high)

    top, bottom = slice(13, 16), slice(0, 3)
    for q in range(len(PAIRS)):
        put(3 * q, 3, main(q, top), main(q, bottom))
    put(240, 8, edge[0:8, :], edge[8:16, :])
    for tile in range(2):
        put(
            248 + 3 * tile,
            3,
            jnp.where(even_z, zfar[tile, top, :], znear[tile, top, :]),
            jnp.where(even_z, zfar[tile, bottom, :], znear[tile, bottom, :]),
        )
        put(
            254 + 3 * tile,
            3,
            jnp.where(even_z, znear[tile, top, :], zfar[tile, top, :]),
            jnp.where(even_z, znear[tile, bottom, :], zfar[tile, bottom, :]),
        )
    near[260:264, :] = jnp.zeros((4, 128), jnp.float32)
    far[260:264, :] = jnp.zeros((4, 128), jnp.float32)


def shifted(value, shift_y, shift_z):
    if shift_y:
        value = pltpu.roll(value, shift_y % 24, 0)
    if shift_z:
        value = pltpu.roll(value, shift_z % 256, 1)
    return value


def step_kernel(
    par,
    post,
    xnear,
    xfar,
    znear,
    zfar,
    ynear,
    yfar,
    dep_a,
    dep_b,
    pops_out,
    fluid,
    partial,
    snear,
    sfar,
    columns,
    field_ext,
    second,
):
    main = reader(par, post, xnear, xfar)
    even_x, even_y, even_z = par[0] == 0, par[1] == 0, par[2] == 0

    def dep(c, k, plane):
        return (dep_a if c < 2 else dep_b)[c % 2, k, plane]

    def y_low(row, count):
        return jnp.where(even_y, yfar[row : row + count, :], ynear[row : row + count, :])

    def y_high(row, count):
        return jnp.where(even_y, ynear[row : row + count, :], yfar[row : row + count, :])

    zero = jnp.zeros((8, 128), jnp.float32)
    for tile in range(2):
        for side in range(2):
            a, b = (zfar, znear) if side == 0 else (znear, zfar)
            columns[side, tile, 0:16, :] = jnp.where(even_z, a[tile], b[tile])
            columns[side, tile, 16:24, :] = zero
            row = 248 + 6 * side + 3 * tile
            columns[side, tile, 16:19, :] = y_high(row, 3)
            columns[side, tile, 21:24, :] = y_low(row, 3)
    lane = lax.broadcasted_iota(jnp.int32, (24, 128), 1)
    for q in range(len(PAIRS)):
        tile, slot = (0, q) if q < FIRST else (1, q - FIRST)
        field_ext[q, 0:16, 0:128] = main(q)
        field_ext[q, 16:24, 0:128] = zero
        field_ext[q, 16:19, 0:128] = y_high(3 * q, 3)
        field_ext[q, 21:24, 0:128] = y_low(3 * q, 3)
        low = pltpu.roll(columns[0, tile], (125 - 3 * slot) % 128, 1)
        high = pltpu.roll(columns[1, tile], (-3 * slot) % 128, 1)
        field_ext[q, :, 128:256] = jnp.where(lane < 64, high, low)

    for plane in range(4):
        for i in range(19):
            cx, cy, cz = SPEEDS[i]
            value = field_ext[INDEX[(i, plane - 1 - cx)]]
            second[i, plane] = shifted(value, cy, cz).reshape(3, 8, 256)

    for plane in range(4):
        rates = INDEX[(SHEAR, plane - 1)]

        def body(t, carry, plane=plane, rates=rates):
            row = pl.multiple_of(t * 8, 8)
            for z in range(2):
                lanes = slice(128 * z, 128 * z + 128)
                rate = field_ext[rates, pl.ds(row, 8), lanes]
                out = relax([second[i, plane, t, :, lanes] for i in range(19)], rate)
                for i in range(19):
                    second[i, plane, t, :, lanes] = out[i]
            return carry

        lax.fori_loop(0, 3, body, 0)

    lane16 = lax.broadcasted_iota(jnp.int32, (16, 128), 1)
    row8 = lax.broadcasted_iota(jnp.int32, (8, 128), 0)
    totals = [[None, None] for _ in range(4)]
    ups, downs = [None] * 4, [None] * 4
    for plane in range(2):
        rho = jx = jy = jz = None

        def add(total, value, sign):
            if sign == 0:
                return total
            if total is None:
                return value if sign > 0 else -value
            return total + value if sign > 0 else total - value

        for i in range(19):
            cx, cy, cz = SPEEDS[i]
            value = shifted(second[i, plane + 1 - cx].reshape(24, 256), cy, cz)
            pops_out[i, plane] = value[0:16, 0:128]
            rho = add(rho, value, 1)
            jx, jy, jz = add(jx, value, cx), add(jy, value, cy), add(jz, value, cz)
        u = [jx / rho, jy / rho, jz / rho]
        for c in range(3):
            fluid[c, plane] = u[c][0:16, 0:128]

        def moved(k, speed):
            s = dep(3, k, plane)
            return [dep(c, k, plane) - speed[c] * s for c in range(3)] + [2.0 * s]

        inner = [u[c][0:16, 0:128] for c in range(3)]
        total = moved(0, inner)
        tops = moved(1, inner)
        bottoms = moved(2, inner)

        def y_ext(k):
            ghosts = []
            for c in range(4):
                row = 240 + 2 * c + plane
                if k == 3:
                    ghost = jnp.where(row8 == 7, jnp.broadcast_to(y_low(row, 1), (8, 128)), 0.0)
                else:
                    ghost = jnp.where(row8 == 0, jnp.broadcast_to(y_high(row, 1), (8, 128)), 0.0)
                ghosts.append(jnp.concatenate([dep(c, k, plane), ghost], 0))
            return ghosts

        def z_ext(k):
            ghosts = []
            for c in range(4):
                spot = DEP_LANE + 2 * c + plane
                if k == 5:
                    ghost = pltpu.roll(columns[0, 1, 0:16, :], (127 - spot) % 128, 1)
                    ghost = jnp.where(lane16 == 127, ghost, 0.0)
                else:
                    ghost = pltpu.roll(columns[1, 1, 0:16, :], (-spot) % 128, 1)
                    ghost = jnp.where(lane16 == 0, ghost, 0.0)
                ghosts.append(jnp.concatenate([dep(c, k, plane), ghost], 1))
            return ghosts

        for k, shift in ((3, 1), (4, 23)):
            v = y_ext(k)
            rows = [v[c] - jnp.where(v[3] != 0.0, u[c][:, 0:128] * v[3], 0.0) for c in range(3)]
            rows.append(2.0 * v[3])
            for c in range(4):
                total[c] = total[c] + pltpu.roll(rows[c], shift, 0)[0:16, :]
        for k, shift in ((5, 1), (6, 255)):
            v = z_ext(k)
            rows = [v[c] - jnp.where(v[3] != 0.0, u[c][0:16, :] * v[3], 0.0) for c in range(3)]
            rows.append(2.0 * v[3])
            for c in range(4):
                total[c] = total[c] + pltpu.roll(rows[c], shift, 1)[:, 0:128]
        for c in range(4):
            totals[c][plane] = total[c]
        if plane == 0:
            downs, held = bottoms, tops
        else:
            ups = tops
            for c in range(4):
                totals[c][0] = totals[c][0] + bottoms[c]
                totals[c][1] = totals[c][1] + held[c]
    for c in range(4):
        partial[c, 0] = totals[c][0]
        partial[c, 1] = totals[c][1]
        snear[c] = jnp.where(even_x, ups[c], downs[c])
        sfar[c] = jnp.where(even_x, downs[c], ups[c])


def pieces(value):
    coarse = value.astype(jnp.bfloat16)
    return coarse, (value - coarse.astype(jnp.float32)).astype(jnp.bfloat16)


def small(value):
    return value.astype(jnp.float32).astype(jnp.bfloat16)


def numbers(rows, width):
    return lax.broadcasted_iota(jnp.int32, (rows, width), 0)


BY_LANE = (((1,), (1,)), ((), ()))


def deposit_kernel(fields, cell, move, mask, mass, velocity, out, picked, keys):
    where = cell[...]
    width = where.shape[1]
    code = small(move[...] * 32 + jnp.right_shift(where, 7))
    spot = small(jnp.bitwise_and(where, 127))
    weight = 0.5 * mask[...].astype(jnp.float32) * mass[...]
    rows = small(numbers(256, width))
    keys[...] = jnp.where(rows == code, jnp.bfloat16(1), jnp.bfloat16(0))
    here = rows[0:128] == spot
    for n, c in enumerate(fields):
        value = weight * velocity[c : c + 1, :] if c < 3 else weight
        for piece, part in enumerate(pieces(value)):
            at = 256 * n + 128 * piece
            picked[at : at + 128, :] = jnp.where(here, part, jnp.bfloat16(0))
    total = lax.dot_general(
        keys[...], picked[...], BY_LANE, preferred_element_type=jnp.float32
    )
    for n in range(2):
        out[n] = total[:, 256 * n : 256 * n + 128] + total[:, 256 * n + 128 : 256 * n + 256]


def edge_rows(mask, mass, velocity, target, code):
    weight = 0.5 * mask[...].astype(jnp.float32) * mass[...]
    width = weight.shape[1]
    values = [weight * velocity[c : c + 1, :] for c in range(3)] + [weight]
    field = jnp.bitwise_and(jnp.right_shift(numbers(16, width), 1), 3)
    chosen = jnp.where(field == 0, values[0], values[1])
    chosen = jnp.where(field == 2, values[2], chosen)
    chosen = jnp.where(field == 3, values[3], chosen)
    chosen = jnp.where(code == target, chosen, 0.0)
    return jnp.concatenate(pieces(chosen), 0)


def z_edge_kernel(cell, move, mask, mass, velocity, out):
    where = cell[...]
    width = where.shape[1]
    low = jnp.right_shift(numbers(16, width), 3)
    target = jnp.where(low == 0, 5 * 128 + 127, 6 * 128)
    code = move[...] * 128 + jnp.bitwise_and(where, 127)
    rows = edge_rows(mask, mass, velocity, target, code)
    line = jnp.where(
        small(numbers(32, width)) == small(jnp.right_shift(where, 7)), jnp.bfloat16(1), jnp.bfloat16(0)
    )
    out[...] = jnp.zeros_like(out)
    out[:, 0:32] = lax.dot_general(line, rows, BY_LANE, preferred_element_type=jnp.float32)


def y_edge_kernel(cell, move, mask, mass, velocity, out, tall):
    where = cell[...]
    width = where.shape[1]
    row = numbers(16, width)
    plane = jnp.bitwise_and(row, 1) * 16
    target = jnp.where(row < 8, 3 * 32 + 15 + plane, 4 * 32 + plane)
    code = move[...] * 32 + jnp.right_shift(where, 7)
    rows = edge_rows(mask, mass, velocity, target, code)
    here = jnp.where(
        small(numbers(128, width)) == small(jnp.bitwise_and(where, 127)), jnp.bfloat16(1), jnp.bfloat16(0)
    )
    total = lax.dot_general(rows, here, BY_LANE, preferred_element_type=jnp.float32)
    out[...] = total[0:16, :] + total[16:32, :]
    for j in range(width // 128):
        for c in range(3):
            tall[c, j : j + 1, :] = velocity[c : c + 1, 128 * j : 128 * j + 128]


def drag_kernel(cell, mask, velocity, fluid, out):
    for group in range(8):
        rows = slice(8 * group, 8 * group + 8)
        where = cell[rows, :]
        lane = jnp.bitwise_and(where, 127)
        line = jnp.right_shift(where, 7)
        picked = [jnp.zeros((8, 128), jnp.float32) for _ in range(3)]
        for r in range(32):
            mine = line == r
            for c in range(3):
                table = jnp.broadcast_to(fluid[c, r : r + 1, :], (8, 128))
                value = jnp.take_along_axis(table, lane, axis=1)
                picked[c] = jnp.where(mine, value, picked[c])
        half = 0.5 * mask[rows, :].astype(jnp.float32)
        for c in range(3):
            old = velocity[c, rows, :]
            new = old + half * (picked[c] - old)
            for r in range(8):
                at = 128 * (8 * group + r)
                out[c : c + 1, at : at + 128] = new[r : r + 1, :]


def swap(value, axis, shifted_by_one):
    count = lax.axis_size(axis)
    pairs = []
    for i in range(count):
        if shifted_by_one:
            pairs.append((i, (i + 1) % count if i % 2 else (i - 1) % count))
        else:
            pairs.append((i, i ^ 1))
    return lax.ppermute(value, axis, pairs)


def both_swaps(near, far, axis):
    far = swap(far, axis, True)
    near = swap(near, axis, False)
    return near, far


def struct(*shape):
    return jax.ShapeDtypeStruct(shape, jnp.float32)


def call(kernel, outs, args, specs=None, scratch=(), flops=1000000, size=1000000):
    single = not isinstance(outs, tuple)
    return pl.pallas_call(
        kernel,
        out_shape=outs,
        in_specs=specs or [VMEM] * len(args),
        out_specs=VMEM if single else (VMEM,) * len(outs),
        scratch_shapes=scratch,
        compiler_params=pltpu.CompilerParams(vmem_limit_bytes=40 << 20),
        cost_estimate=pl.CostEstimate(flops=flops, bytes_accessed=size, transcendentals=0),
    )(*args)


def body(populations, shear_rate, part_cell, part_move, part_mask, part_velocity, part_mass):
    par = jnp.stack([lax.axis_index(a) % 2 for a in ("gx", "gy", "gz")]).astype(jnp.int32)
    count = part_cell.shape[0]
    flat = (1, count)
    particles = (
        part_cell.reshape(flat),
        part_move.reshape(flat),
        part_mask.reshape(flat),
        part_mass.reshape(flat),
        part_velocity,
    )

    post, near, far = call(
        collide_kernel,
        (struct(20, 2, 16, 128), struct(20, 16, 128), struct(20, 16, 128)),
        (
            par,
            pltpu.with_memory_space_constraint(populations, pltpu.HBM),
            pltpu.with_memory_space_constraint(shear_rate, pltpu.HBM),
        ),
        [SMEM, HBM, HBM],
        [pltpu.VMEM((19, 2, 16, 128), jnp.float32), pltpu.SemaphoreType.DMA((5,))],
    )
    xnear, xfar = both_swaps(near, far, "gx")

    edge = call(z_edge_kernel, struct(32, 128), particles)
    near, far = call(
        z_pack_kernel,
        (struct(2, 16, 128), struct(2, 16, 128)),
        (par, post, xnear, xfar, edge),
        [SMEM] + [VMEM] * 4,
    )
    znear, zfar = both_swaps(near, far, "gz")

    edge, velocity_tall = call(
        y_edge_kernel, (struct(16, 128), struct(3, count // 128, 128)), particles
    )
    scratch = [pltpu.VMEM((512, count), jnp.bfloat16), pltpu.VMEM((256, count), jnp.bfloat16)]
    deposits = [
        call(
            functools.partial(deposit_kernel, fields),
            struct(2, 256, 128),
            particles,
            scratch=scratch,
            flops=2000000000,
        ).reshape(2, 8, 2, 16, 128)
        for fields in ((0, 1), (2, 3))
    ]
    near, far = call(
        y_pack_kernel,
        (struct(Y_ROWS, 128), struct(Y_ROWS, 128)),
        (par, post, xnear, xfar, znear, zfar, edge),
        [SMEM] + [VMEM] * 6,
    )
    ynear, yfar = both_swaps(near, far, "gy")

    populations_out, fluid, partial, near, far = call(
        step_kernel,
        (
            struct(19, 2, 16, 128),
            struct(3, 2, 16, 128),
            struct(4, 2, 16, 128),
            struct(4, 16, 128),
            struct(4, 16, 128),
        ),
        (par, post, xnear, xfar, znear, zfar, ynear, yfar, *deposits),
        [SMEM] + [VMEM] * 9,
        [
            pltpu.VMEM((2, 2, 24, 128), jnp.float32),
            pltpu.VMEM((len(PAIRS), 24, 256), jnp.float32),
            pltpu.VMEM((19, 4, 3, 8, 256), jnp.float32),
        ],
        flops=20000000,
    )
    snear, sfar = both_swaps(near, far, "gx")

    tall = (count // 128, 128)
    velocity_out = call(
        drag_kernel,
        struct(3, count),
        (
            part_cell.reshape(tall),
            part_mask.reshape(tall),
            velocity_tall,
            fluid.reshape(3, 32, 128),
        ),
    )

    even = par[0] == 0
    upper = lax.broadcasted_iota(jnp.int32, partial.shape, 1) == 1
    sources = partial + jnp.where(upper == even, snear[:, None], sfar[:, None])
    return populations_out, sources, velocity_out


def solution(mesh):
    placed = (
        P(None, "gx", "gy", "gz"),
        P("gx", "gy", "gz"),
        P(("gx", "gy", "gz")),
        P(("gx", "gy", "gz")),
        P(("gx", "gy", "gz")),
        P(None, ("gx", "gy", "gz")),
        P(("gx", "gy", "gz")),
    )
    return jax.shard_map(
        body,
        mesh=mesh,
        in_specs=placed,
        out_specs=(
            P(None, "gx", "gy", "gz"),
            P(None, "gx", "gy", "gz"),
            P(None, ("gx", "gy", "gz")),
        ),
        check_vma=False,
    )
```

```python
import functools

import jax
import jax.numpy as jnp
from jax import lax
from jax.experimental import pallas as pl
from jax.experimental.pallas import tpu as pltpu
from jax.sharding import PartitionSpec as P

SPEEDS = (
    (0, 0, 0),
    (1, 0, 0),
    (-1, 0, 0),
    (0, 1, 0),
    (0, -1, 0),
    (0, 0, 1),
    (0, 0, -1),
    (1, 1, 0),
    (-1, -1, 0),
    (1, -1, 0),
    (-1, 1, 0),
    (1, 0, 1),
    (-1, 0, -1),
    (1, 0, -1),
    (-1, 0, 1),
    (0, 1, 1),
    (0, -1, -1),
    (0, 1, -1),
    (0, -1, 1),
)
SHEAR = 19
UP = [i for i in range(19) if SPEEDS[i][0] == 1]
FLAT = [i for i in range(19) if SPEEDS[i][0] == 0]
DOWN = [i for i in range(19) if SPEEDS[i][0] == -1]
X_LOW = [(f, -1) for f in UP + FLAT + [SHEAR]] + [(f, -2) for f in UP]
X_HIGH = [(f, 2) for f in DOWN + FLAT + [SHEAR]] + [(f, 3) for f in DOWN]
PAIRS = X_LOW + [(f, 0) for f in range(20)] + [(f, 1) for f in range(20)] + X_HIGH
INDEX = {pair: q for q, pair in enumerate(PAIRS)}
FIRST = 42
DEP_LANE = 3 * (len(PAIRS) - FIRST)
Y_ROWS = 264
VMEM = pl.BlockSpec(memory_space=pltpu.VMEM)
SMEM = pl.BlockSpec(memory_space=pltpu.SMEM)
HBM = pl.BlockSpec(memory_space=pltpu.HBM)


def relax(f, shear):
    s1, s2, s3 = f[1] + f[2], f[3] + f[4], f[5] + f[6]
    d1, d2, d3 = f[1] - f[2], f[3] - f[4], f[5] - f[6]
    e1, e2, e3 = f[7] + f[8], f[9] + f[10], f[11] + f[12]
    e4, e5, e6 = f[13] + f[14], f[15] + f[16], f[17] + f[18]
    g1, g2, g3 = f[7] - f[8], f[9] - f[10], f[11] - f[12]
    g4, g5, g6 = f[13] - f[14], f[15] - f[16], f[17] - f[18]
    exy, exz, eyz = e1 + e2, e3 + e4, e5 + e6
    s23, m23 = s2 + s3, s2 - s3
    axes = s1 + s23
    exx = exy + exz
    edges = exx + eyz
    rho = f[0] + axes + edges
    gp, gm = g1 + g2, g1 - g2
    hp, hm = g3 + g4, g3 - g4
    kp, km = g5 + g6, g5 - g6
    gx, gy, gz = gp + hp, gm + kp, hm + km
    jx, jy, jz = d1 + gx, d2 + gy, d3 + gz
    inv = 1.0 / rho
    ux, uy, uz = jx * inv, jy * inv, jz * inv
    xx, yy, zz = jx * ux, jy * uy, jz * uz
    sq = xx + yy + zz
    n1 = 8.0 * edges - 11.0 * axes - 30.0 * f[0] + (11.0 * rho - 19.0 * sq)
    n2 = 12.0 * f[0] - 4.0 * axes + edges - (3.0 * rho - 5.5 * sq)
    a9 = 2.0 * s1 - s23
    b9 = exx - 2.0 * eyz
    q9 = 3.0 * xx - sq
    b11 = exy - exz
    q11 = yy - zz
    t1 = n1 * (1.19 / 2394.0)
    t2 = n2 * (1.4 / 252.0)
    t4 = (gx - 4.0 * d1 + (2.0 / 3.0) * jx) * (1.2 / 40.0)
    t6 = (gy - 4.0 * d2 + (2.0 / 3.0) * jy) * (1.2 / 40.0)
    t8 = (gz - 4.0 * d3 + (2.0 / 3.0) * jz) * (1.2 / 40.0)
    t9 = (a9 + b9 - q9) * (shear * (1.0 / 36.0))
    t10 = (b9 - 2.0 * a9 + 0.5 * q9) * (1.4 / 72.0)
    t11 = (m23 + b11 - q11) * (shear * (1.0 / 12.0))
    t12 = (b11 - 2.0 * m23 + 0.5 * q11) * (1.4 / 24.0)
    quarter = shear * 0.25
    t13 = (e1 - e2 - jx * uy) * quarter
    t14 = (e5 - e6 - jy * uz) * quarter
    t15 = (e3 - e4 - jx * uz) * quarter
    t16 = (gp - hp) * (1.98 / 8.0)
    t17 = (kp - gm) * (1.98 / 8.0)
    t18 = (hm - km) * (1.98 / 8.0)
    axis = -11.0 * t1 - 4.0 * t2
    edge = 8.0 * t1 + t2
    p9 = t9 - 2.0 * t10
    p11 = t11 - 2.0 * t12
    r9 = t9 + t10
    r11 = t11 + t12
    out = [None] * 19
    out[0] = f[0] + 30.0 * t1 - 12.0 * t2

    def put(i, even, odd):
        out[i] = f[i] - (even + odd)
        out[i + 1] = f[i + 1] - (even - odd)

    put(1, axis + 2.0 * p9, -4.0 * t4)
    put(3, axis - p9 + p11, -4.0 * t6)
    put(5, axis - p9 - p11, -4.0 * t8)
    vxy, vxz, vyz = edge + r9 + r11, edge + r9 - r11, edge - 2.0 * r9
    put(7, vxy + t13, t4 + t6 + (t16 - t17))
    put(9, vxy - t13, t4 - t6 + (t16 + t17))
    put(11, vxz + t15, t4 + t8 - (t16 - t18))
    put(13, vxz - t15, t4 - t8 - (t16 + t18))
    put(15, vyz + t14, t6 + t8 + (t17 - t18))
    put(17, vyz - t14, t6 - t8 + (t17 + t18))
    return out


def collide_kernel(par, pops_hbm, shear_hbm, *refs):
    given, (post, near, far), held = refs[0:5], refs[5:8], refs[8:13]
    pops, sems = refs[13:]
    even = par[0] == 0
    rate_copy = pltpu.make_async_copy(shear_hbm, post.at[SHEAR], sems.at[4])
    rate_copy.start()
    copies = []
    for plane in range(2):
        for half in range(2):
            rows = slice(8 * half, 8 * half + 8)
            copy = pltpu.make_async_copy(
                pops_hbm.at[:, plane, rows, :], pops.at[:, plane, rows, :], sems.at[2 * plane + half]
            )
            copy.start()
            copies.append(copy)
    for n in range(5):
        copy = pltpu.make_async_copy(given[n], held[n], sems.at[5 + n])
        copy.start()
        copies.append(copy)
    rate_copy.wait()
    for plane in range(2):
        for half in range(2):
            rows = slice(8 * half, 8 * half + 8)
            copies[2 * plane + half].wait()
            rate = post[SHEAR, plane, rows, :]
            out = relax([pops[i, plane, rows, :] for i in range(19)], rate)
            for i in range(19):
                post[i, plane, rows, :] = out[i]

    for slot in range(20):
        up = post[X_LOW[slot][0], X_LOW[slot][1] + 2]
        down = post[X_HIGH[slot][0], X_HIGH[slot][1] - 2]
        near[slot] = jnp.where(even, up, down)
        far[slot] = jnp.where(even, down, up)
    for copy in copies[4:]:
        copy.wait()


def reader(par, post, near, far):
    even = par[0] == 0

    def main(q, rows=slice(0, 16)):
        if q < 20:
            return jnp.where(even, far[q, rows, :], near[q, rows, :])
        if q >= 60:
            return jnp.where(even, near[q - 60, rows, :], far[q - 60, rows, :])
        field, plane = PAIRS[q]
        return post[field, plane, rows, :]

    return main


def z_pack_kernel(par, post, xnear, xfar, edge, near, far):
    main = reader(par, post, xnear, xfar)
    even = par[2] == 0
    lane = lax.broadcasted_iota(jnp.int32, (16, 128), 1)
    for tile in range(2):
        high = jnp.zeros((16, 128), jnp.float32)
        low = jnp.zeros((16, 128), jnp.float32)
        for slot in range(FIRST if tile == 0 else len(PAIRS) - FIRST):
            value = main(tile * FIRST + slot)
            mine = (lane >= 3 * slot) & (lane < 3 * slot + 3)
            high = jnp.where(mine, pltpu.roll(value, (3 * slot + 3) % 128, 1), high)
            low = jnp.where(mine, pltpu.roll(value, 3 * slot, 1), low)
        if tile == 1:
            sums = edge[...] + pltpu.roll(edge[...], 112, 1)
            odd = jnp.bitwise_and(lane - DEP_LANE, 1) == 1
            ours = (lane >= DEP_LANE) & (lane < DEP_LANE + 8)
            for shift in (DEP_LANE, DEP_LANE - 8):
                placed = pltpu.roll(sums, shift, 1)
                placed = jnp.where(odd, placed[16:32, :], placed[0:16, :])
                if shift == DEP_LANE:
                    high = jnp.where(ours, placed, high)
                else:
                    low = jnp.where(ours, placed, low)
        near[tile] = jnp.where(even, high, low)
        far[tile] = jnp.where(even, low, high)


def y_pack_kernel(par, post, xnear, xfar, znear, zfar, edge, near, far):
    main = reader(par, post, xnear, xfar)
    even = par[1] == 0
    even_z = par[2] == 0

    def put(row, count, high, low):
        near[row : row + count, :] = jnp.where(even, high, low)
        far[row : row + count, :] = jnp.where(even, low, high)

    top, bottom = slice(13, 16), slice(0, 3)
    for q in range(len(PAIRS)):
        put(3 * q, 3, main(q, top), main(q, bottom))
    put(240, 8, edge[0:8, :], edge[8:16, :])
    for tile in range(2):
        put(
            248 + 3 * tile,
            3,
            jnp.where(even_z, zfar[tile, top, :], znear[tile, top, :]),
            jnp.where(even_z, zfar[tile, bottom, :], znear[tile, bottom, :]),
        )
        put(
            254 + 3 * tile,
            3,
            jnp.where(even_z, znear[tile, top, :], zfar[tile, top, :]),
            jnp.where(even_z, znear[tile, bottom, :], zfar[tile, bottom, :]),
        )
    near[260:264, :] = jnp.zeros((4, 128), jnp.float32)
    far[260:264, :] = jnp.zeros((4, 128), jnp.float32)


def shifted(value, shift_y, shift_z):
    if shift_y:
        value = pltpu.roll(value, shift_y % 24, 0)
    if shift_z:
        value = pltpu.roll(value, shift_z % 256, 1)
    return value


def sided(first, second, tile):
    tile, slot = tile
    low = pltpu.roll(first[tile], (125 - 3 * slot) % 128, 1)
    high = pltpu.roll(second[tile], (-3 * slot) % 128, 1)
    lane = lax.broadcasted_iota(jnp.int32, low.shape, 1)
    return jnp.where(lane < 64, high, low)


def column_spot(q):
    return (0, q) if q < FIRST else (1, q - FIRST)


def collide_rows(rate_of, fields, plane, index):
    for z in range(2):
        lanes = slice(128 * z, 128 * z + 128)
        at = index + (slice(None), lanes)
        out = relax([fields[(i, plane) + at] for i in range(19)], rate_of(lanes))
        for i in range(19):
            fields[(i, plane) + at] = out[i]


def inner_kernel(par, post, xnear, xfar, znear, zfar, field_ext, second):
    main = reader(par, post, xnear, xfar)
    even_z = par[2] == 0
    low = [jnp.where(even_z, zfar[t], znear[t]) for t in range(2)]
    high = [jnp.where(even_z, znear[t], zfar[t]) for t in range(2)]
    for q in range(len(PAIRS)):
        field_ext[q, :, 0:128] = main(q)
        field_ext[q, :, 128:256] = sided(low, high, column_spot(q))
    for plane in range(4):
        for i in range(19):
            cx, cy, cz = SPEEDS[i]
            value = field_ext[INDEX[(i, plane - 1 - cx)]]
            if cy:
                value = pltpu.roll(value, cy % 16, 0)
            if cz:
                value = pltpu.roll(value, cz % 256, 1)
            second[i, plane] = value.reshape(2, 8, 256)
    for plane in range(4):
        rates = INDEX[(SHEAR, plane - 1)]

        def body(t, carry, plane=plane, rates=rates):
            row = pl.multiple_of(t * 8, 8)
            collide_rows(lambda lanes: field_ext[rates, pl.ds(row, 8), lanes], second, plane, (t,))
            return carry

        lax.fori_loop(0, 2, body, 0)


def step_kernel(
    par,
    field_ext,
    middle,
    znear,
    zfar,
    ynear,
    yfar,
    dep_a,
    dep_b,
    pops_out,
    fluid,
    partial,
    snear,
    sfar,
    window,
    rim,
):
    even_x, even_y, even_z = par[0] == 0, par[1] == 0, par[2] == 0

    def dep(c, k, plane):
        return (dep_a if c < 2 else dep_b)[c % 2, k, plane]

    def y_low(row, count):
        return jnp.where(even_y, yfar[row : row + count, :], ynear[row : row + count, :])

    def y_high(row, count):
        return jnp.where(even_y, ynear[row : row + count, :], yfar[row : row + count, :])

    pad = jnp.zeros((2, 128), jnp.float32)
    packed = [
        [
            jnp.concatenate([y_high(row, 3), y_low(row, 3), pad], 0)
            for row in (248 + 6 * side, 251 + 6 * side)
        ]
        for side in range(2)
    ]
    for q in range(len(PAIRS)):
        window[q, 0:8, :] = field_ext[q, 8:16, :]
        window[q, 8:11, 0:128] = y_high(3 * q, 3)
        window[q, 11:14, 0:128] = y_low(3 * q, 3)
        window[q, 8:14, 128:256] = sided(packed[0], packed[1], column_spot(q))[0:6, :]
        window[q, 14:16, :] = field_ext[q, 0:2, :]

    for plane in range(4):
        rates = INDEX[(SHEAR, plane - 1)]
        for i in range(19):
            cx, cy, cz = SPEEDS[i]
            value = window[INDEX[(i, plane - 1 - cx)], 7 - cy : 15 - cy, :]
            if cz:
                value = pltpu.roll(value, cz % 256, 1)
            rim[i, plane] = value
        collide_rows(lambda lanes, rates=rates: window[rates, 7:15, lanes], rim, plane, ())

    row_of = lax.broadcasted_iota(jnp.int32, (8, 256), 0)

    def collided(i, plane):
        down, up = pltpu.roll(rim[i, plane], 1, 0), pltpu.roll(rim[i, plane], 7, 0)
        return jnp.concatenate(
            [
                jnp.where(row_of == 0, down, middle[i, plane, 0]),
                jnp.where(row_of == 7, up, middle[i, plane, 1]),
                jnp.where(row_of < 4, up, down),
            ],
            0,
        )

    lane16 = lax.broadcasted_iota(jnp.int32, (16, 128), 1)
    row8 = lax.broadcasted_iota(jnp.int32, (8, 128), 0)
    totals = [[None, None] for _ in range(4)]
    ups, downs = [None] * 4, [None] * 4
    for plane in range(2):
        rho = jx = jy = jz = None

        def add(total, value, sign):
            if sign == 0:
                return total
            if total is None:
                return value if sign > 0 else -value
            return total + value if sign > 0 else total - value

        for i in range(19):
            cx, cy, cz = SPEEDS[i]
            value = shifted(collided(i, plane + 1 - cx), cy, cz)
            pops_out[i, plane] = value[0:16, 0:128]
            rho = add(rho, value, 1)
            jx, jy, jz = add(jx, value, cx), add(jy, value, cy), add(jz, value, cz)
        u = [jx / rho, jy / rho, jz / rho]
        for c in range(3):
            fluid[c, plane] = u[c][0:16, 0:128]

        def moved(k, speed):
            s = dep(3, k, plane)
            return [dep(c, k, plane) - speed[c] * s for c in range(3)] + [2.0 * s]

        inner = [u[c][0:16, 0:128] for c in range(3)]
        total = moved(0, inner)
        tops = moved(1, inner)
        bottoms = moved(2, inner)

        def y_ext(k):
            ghosts = []
            for c in range(4):
                row = 240 + 2 * c + plane
                if k == 3:
                    ghost = jnp.where(row8 == 7, jnp.broadcast_to(y_low(row, 1), (8, 128)), 0.0)
                else:
                    ghost = jnp.where(row8 == 0, jnp.broadcast_to(y_high(row, 1), (8, 128)), 0.0)
                ghosts.append(jnp.concatenate([dep(c, k, plane), ghost], 0))
            return ghosts

        def z_ext(k):
            ghosts = []
            for c in range(4):
                spot = DEP_LANE + 2 * c + plane
                if k == 5:
                    ghost = jnp.where(even_z, zfar[1], znear[1])
                    ghost = pltpu.roll(ghost, (127 - spot) % 128, 1)
                    ghost = jnp.where(lane16 == 127, ghost, 0.0)
                else:
                    ghost = jnp.where(even_z, znear[1], zfar[1])
                    ghost = pltpu.roll(ghost, (-spot) % 128, 1)
                    ghost = jnp.where(lane16 == 0, ghost, 0.0)
                ghosts.append(jnp.concatenate([dep(c, k, plane), ghost], 1))
            return ghosts

        for k, shift in ((3, 1), (4, 23)):
            v = y_ext(k)
            rows = [v[c] - jnp.where(v[3] != 0.0, u[c][:, 0:128] * v[3], 0.0) for c in range(3)]
            rows.append(2.0 * v[3])
            for c in range(4):
                total[c] = total[c] + pltpu.roll(rows[c], shift, 0)[0:16, :]
        for k, shift in ((5, 1), (6, 255)):
            v = z_ext(k)
            rows = [v[c] - jnp.where(v[3] != 0.0, u[c][0:16, :] * v[3], 0.0) for c in range(3)]
            rows.append(2.0 * v[3])
            for c in range(4):
                total[c] = total[c] + pltpu.roll(rows[c], shift, 1)[:, 0:128]
        for c in range(4):
            totals[c][plane] = total[c]
        if plane == 0:
            downs, held = bottoms, tops
        else:
            ups = tops
            for c in range(4):
                totals[c][0] = totals[c][0] + bottoms[c]
                totals[c][1] = totals[c][1] + held[c]
    for c in range(4):
        partial[c, 0] = totals[c][0]
        partial[c, 1] = totals[c][1]
        snear[c] = jnp.where(even_x, ups[c], downs[c])
        sfar[c] = jnp.where(even_x, downs[c], ups[c])


def pieces(value):
    coarse = value.astype(jnp.bfloat16)
    return coarse, (value - coarse.astype(jnp.float32)).astype(jnp.bfloat16)


def small(value):
    return value.astype(jnp.float32).astype(jnp.bfloat16)


def numbers(rows, width):
    return lax.broadcasted_iota(jnp.int32, (rows, width), 0)


BY_LANE = (((1,), (1,)), ((), ()))


def deposit_kernel(fields, cell, move, mask, mass, velocity, out, picked, keys):
    where = cell[...]
    width = where.shape[1]
    code = small(move[...] * 32 + jnp.right_shift(where, 7))
    spot = small(jnp.bitwise_and(where, 127))
    weight = 0.5 * mask[...].astype(jnp.float32) * mass[...]
    rows = small(numbers(256, width))
    keys[...] = jnp.where(rows == code, jnp.bfloat16(1), jnp.bfloat16(0))
    here = rows[0:128] == spot
    for n, c in enumerate(fields):
        value = weight * velocity[c : c + 1, :] if c < 3 else weight
        for piece, part in enumerate(pieces(value)):
            at = 256 * n + 128 * piece
            picked[at : at + 128, :] = jnp.where(here, part, jnp.bfloat16(0))
    total = lax.dot_general(
        keys[...], picked[...], BY_LANE, preferred_element_type=jnp.float32
    )
    for n in range(2):
        out[n] = total[:, 256 * n : 256 * n + 128] + total[:, 256 * n + 128 : 256 * n + 256]


def edge_rows(mask, mass, velocity, target, code):
    weight = 0.5 * mask[...].astype(jnp.float32) * mass[...]
    width = weight.shape[1]
    values = [weight * velocity[c : c + 1, :] for c in range(3)] + [weight]
    field = jnp.bitwise_and(jnp.right_shift(numbers(16, width), 1), 3)
    chosen = jnp.where(field == 0, values[0], values[1])
    chosen = jnp.where(field == 2, values[2], chosen)
    chosen = jnp.where(field == 3, values[3], chosen)
    chosen = jnp.where(code == target, chosen, 0.0)
    return jnp.concatenate(pieces(chosen), 0)


def z_edge_kernel(cell, move, mask, mass, velocity, out):
    where = cell[...]
    width = where.shape[1]
    low = jnp.right_shift(numbers(16, width), 3)
    target = jnp.where(low == 0, 5 * 128 + 127, 6 * 128)
    code = move[...] * 128 + jnp.bitwise_and(where, 127)
    rows = edge_rows(mask, mass, velocity, target, code)
    line = jnp.where(
        small(numbers(32, width)) == small(jnp.right_shift(where, 7)), jnp.bfloat16(1), jnp.bfloat16(0)
    )
    out[...] = jnp.zeros_like(out)
    out[:, 0:32] = lax.dot_general(line, rows, BY_LANE, preferred_element_type=jnp.float32)


def y_edge_kernel(cell, move, mask, mass, velocity, out, tall):
    where = cell[...]
    width = where.shape[1]
    row = numbers(16, width)
    plane = jnp.bitwise_and(row, 1) * 16
    target = jnp.where(row < 8, 3 * 32 + 15 + plane, 4 * 32 + plane)
    code = move[...] * 32 + jnp.right_shift(where, 7)
    rows = edge_rows(mask, mass, velocity, target, code)
    here = jnp.where(
        small(numbers(128, width)) == small(jnp.bitwise_and(where, 127)), jnp.bfloat16(1), jnp.bfloat16(0)
    )
    total = lax.dot_general(rows, here, BY_LANE, preferred_element_type=jnp.float32)
    out[...] = total[0:16, :] + total[16:32, :]
    for j in range(width // 128):
        for c in range(3):
            tall[c, j : j + 1, :] = velocity[c : c + 1, 128 * j : 128 * j + 128]


def drag_kernel(cell, mask, velocity, fluid, out):
    for group in range(8):
        rows = slice(8 * group, 8 * group + 8)
        where = cell[rows, :]
        lane = jnp.bitwise_and(where, 127)
        line = jnp.right_shift(where, 7)
        picked = [jnp.zeros((8, 128), jnp.float32) for _ in range(3)]
        for r in range(32):
            mine = line == r
            for c in range(3):
                table = jnp.broadcast_to(fluid[c, r : r + 1, :], (8, 128))
                value = jnp.take_along_axis(table, lane, axis=1)
                picked[c] = jnp.where(mine, value, picked[c])
        half = 0.5 * mask[rows, :].astype(jnp.float32)
        for c in range(3):
            old = velocity[c, rows, :]
            new = old + half * (picked[c] - old)
            for r in range(8):
                at = 128 * (8 * group + r)
                out[c : c + 1, at : at + 128] = new[r : r + 1, :]


def swap(value, axis, shifted_by_one):
    count = lax.axis_size(axis)
    pairs = []
    for i in range(count):
        if shifted_by_one:
            pairs.append((i, (i + 1) % count if i % 2 else (i - 1) % count))
        else:
            pairs.append((i, i ^ 1))
    return lax.ppermute(value, axis, pairs)


def both_swaps(near, far, axis):
    far = swap(far, axis, True)
    near = swap(near, axis, False)
    return near, far


def struct(*shape):
    return jax.ShapeDtypeStruct(shape, jnp.float32)


def call(kernel, outs, args, specs=None, scratch=(), flops=1000000, vmem=40):
    single = not isinstance(outs, tuple)
    return pl.pallas_call(
        kernel,
        out_shape=outs,
        in_specs=specs or [VMEM] * len(args),
        out_specs=VMEM if single else (VMEM,) * len(outs),
        scratch_shapes=scratch,
        compiler_params=pltpu.CompilerParams(vmem_limit_bytes=vmem << 20),
        cost_estimate=pl.CostEstimate(flops=flops, bytes_accessed=1000000, transcendentals=0),
    )(*args)


def body(populations, shear_rate, part_cell, part_move, part_mask, part_velocity, part_mass):
    par = jnp.stack([lax.axis_index(a) % 2 for a in ("gx", "gy", "gz")]).astype(jnp.int32)
    count = part_cell.shape[0]
    flat = (1, count)
    particles = (
        part_cell.reshape(flat),
        part_move.reshape(flat),
        part_mask.reshape(flat),
        part_mass.reshape(flat),
        part_velocity,
    )

    post, near, far, *particles = call(
        collide_kernel,
        (struct(20, 2, 16, 128), struct(20, 16, 128), struct(20, 16, 128))
        + tuple(jax.ShapeDtypeStruct(p.shape, p.dtype) for p in particles),
        (par,)
        + tuple(
            pltpu.with_memory_space_constraint(a, pltpu.HBM)
            for a in (populations, shear_rate, *particles)
        ),
        [SMEM] + [HBM] * 7,
        [pltpu.VMEM((19, 2, 16, 128), jnp.float32), pltpu.SemaphoreType.DMA((10,))],
    )
    xnear, xfar = both_swaps(near, far, "gx")

    edge = call(z_edge_kernel, struct(32, 128), particles)
    near, far = call(
        z_pack_kernel,
        (struct(2, 16, 128), struct(2, 16, 128)),
        (par, post, xnear, xfar, edge),
        [SMEM] + [VMEM] * 4,
    )
    znear, zfar = both_swaps(near, far, "gz")

    edge, velocity_tall = call(
        y_edge_kernel, (struct(16, 128), struct(3, count // 128, 128)), particles
    )
    scratch = [pltpu.VMEM((512, count), jnp.bfloat16), pltpu.VMEM((256, count), jnp.bfloat16)]
    deposits = [
        call(
            functools.partial(deposit_kernel, fields),
            struct(2, 256, 128),
            particles,
            scratch=scratch,
            flops=2000000000,
        ).reshape(2, 8, 2, 16, 128)
        for fields in ((0, 1), (2, 3))
    ]
    near, far = call(
        y_pack_kernel,
        (struct(Y_ROWS, 128), struct(Y_ROWS, 128)),
        (par, post, xnear, xfar, znear, zfar, edge),
        [SMEM] + [VMEM] * 6,
    )
    ynear, yfar = both_swaps(near, far, "gy")

    field_ext, inner = call(
        inner_kernel,
        (struct(len(PAIRS), 16, 256), struct(19, 4, 2, 8, 256)),
        (par, post, xnear, xfar, znear, zfar),
        [SMEM] + [VMEM] * 5,
        flops=20000000,
    )
    populations_out, fluid, partial, near, far = call(
        step_kernel,
        (
            struct(19, 2, 16, 128),
            struct(3, 2, 16, 128),
            struct(4, 2, 16, 128),
            struct(4, 16, 128),
            struct(4, 16, 128),
        ),
        (par, field_ext, inner, znear, zfar, ynear, yfar, *deposits),
        [SMEM] + [VMEM] * 8,
        [
            pltpu.VMEM((len(PAIRS), 16, 256), jnp.float32),
            pltpu.VMEM((19, 4, 8, 256), jnp.float32),
        ],
        flops=20000000,
    )
    snear, sfar = both_swaps(near, far, "gx")

    tall = (count // 128, 128)
    velocity_out = call(
        drag_kernel,
        struct(3, count),
        (
            particles[0].reshape(tall),
            particles[2].reshape(tall),
            velocity_tall,
            fluid.reshape(3, 32, 128),
        ),
    )

    even = par[0] == 0
    upper = lax.broadcasted_iota(jnp.int32, partial.shape, 1) == 1
    sources = partial + jnp.where(upper == even, snear[:, None], sfar[:, None])
    return populations_out, sources, velocity_out


def solution(mesh):
    placed = (
        P(None, "gx", "gy", "gz"),
        P("gx", "gy", "gz"),
        P(("gx", "gy", "gz")),
        P(("gx", "gy", "gz")),
        P(("gx", "gy", "gz")),
        P(None, ("gx", "gy", "gz")),
        P(("gx", "gy", "gz")),
    )
    return jax.shard_map(
        body,
        mesh=mesh,
        in_specs=placed,
        out_specs=(
            P(None, "gx", "gy", "gz"),
            P(None, "gx", "gy", "gz"),
            P(None, ("gx", "gy", "gz")),
        ),
        check_vma=False,
    )
```

```python
import functools

import jax
import jax.numpy as jnp
from jax import lax
from jax.experimental import pallas as pl
from jax.experimental.pallas import tpu as pltpu
from jax.sharding import PartitionSpec as P

SPEEDS = (
    (0, 0, 0),
    (1, 0, 0),
    (-1, 0, 0),
    (0, 1, 0),
    (0, -1, 0),
    (0, 0, 1),
    (0, 0, -1),
    (1, 1, 0),
    (-1, -1, 0),
    (1, -1, 0),
    (-1, 1, 0),
    (1, 0, 1),
    (-1, 0, -1),
    (1, 0, -1),
    (-1, 0, 1),
    (0, 1, 1),
    (0, -1, -1),
    (0, 1, -1),
    (0, -1, 1),
)
SHEAR = 19
UP = [i for i in range(19) if SPEEDS[i][0] == 1]
FLAT = [i for i in range(19) if SPEEDS[i][0] == 0]
DOWN = [i for i in range(19) if SPEEDS[i][0] == -1]
X_LOW = [(f, -1) for f in UP + FLAT + [SHEAR]] + [(f, -2) for f in UP]
X_HIGH = [(f, 2) for f in DOWN + FLAT + [SHEAR]] + [(f, 3) for f in DOWN]
PAIRS = X_LOW + [(f, 0) for f in range(20)] + [(f, 1) for f in range(20)] + X_HIGH
INDEX = {pair: q for q, pair in enumerate(PAIRS)}
FIRST = 42
DEP_LANE = 3 * (len(PAIRS) - FIRST)
Y_ROWS = 264
VMEM = pl.BlockSpec(memory_space=pltpu.VMEM)
SMEM = pl.BlockSpec(memory_space=pltpu.SMEM)
HBM = pl.BlockSpec(memory_space=pltpu.HBM)


def relax(f, shear):
    s1, s2, s3 = f[1] + f[2], f[3] + f[4], f[5] + f[6]
    d1, d2, d3 = f[1] - f[2], f[3] - f[4], f[5] - f[6]
    e1, e2, e3 = f[7] + f[8], f[9] + f[10], f[11] + f[12]
    e4, e5, e6 = f[13] + f[14], f[15] + f[16], f[17] + f[18]
    g1, g2, g3 = f[7] - f[8], f[9] - f[10], f[11] - f[12]
    g4, g5, g6 = f[13] - f[14], f[15] - f[16], f[17] - f[18]
    exy, exz, eyz = e1 + e2, e3 + e4, e5 + e6
    s23, m23 = s2 + s3, s2 - s3
    axes = s1 + s23
    exx = exy + exz
    edges = exx + eyz
    rho = f[0] + axes + edges
    gp, gm = g1 + g2, g1 - g2
    hp, hm = g3 + g4, g3 - g4
    kp, km = g5 + g6, g5 - g6
    gx, gy, gz = gp + hp, gm + kp, hm + km
    jx, jy, jz = d1 + gx, d2 + gy, d3 + gz
    inv = 1.0 / rho
    ux, uy, uz = jx * inv, jy * inv, jz * inv
    xx, yy, zz = jx * ux, jy * uy, jz * uz
    sq = xx + yy + zz
    n1 = 8.0 * edges - 11.0 * axes - 30.0 * f[0] + (11.0 * rho - 19.0 * sq)
    n2 = 12.0 * f[0] - 4.0 * axes + edges - (3.0 * rho - 5.5 * sq)
    a9 = 2.0 * s1 - s23
    b9 = exx - 2.0 * eyz
    q9 = 3.0 * xx - sq
    b11 = exy - exz
    q11 = yy - zz
    t1 = n1 * (1.19 / 2394.0)
    t2 = n2 * (1.4 / 252.0)
    t4 = (gx - 4.0 * d1 + (2.0 / 3.0) * jx) * (1.2 / 40.0)
    t6 = (gy - 4.0 * d2 + (2.0 / 3.0) * jy) * (1.2 / 40.0)
    t8 = (gz - 4.0 * d3 + (2.0 / 3.0) * jz) * (1.2 / 40.0)
    t9 = (a9 + b9 - q9) * (shear * (1.0 / 36.0))
    t10 = (b9 - 2.0 * a9 + 0.5 * q9) * (1.4 / 72.0)
    t11 = (m23 + b11 - q11) * (shear * (1.0 / 12.0))
    t12 = (b11 - 2.0 * m23 + 0.5 * q11) * (1.4 / 24.0)
    quarter = shear * 0.25
    t13 = (e1 - e2 - jx * uy) * quarter
    t14 = (e5 - e6 - jy * uz) * quarter
    t15 = (e3 - e4 - jx * uz) * quarter
    t16 = (gp - hp) * (1.98 / 8.0)
    t17 = (kp - gm) * (1.98 / 8.0)
    t18 = (hm - km) * (1.98 / 8.0)
    axis = -11.0 * t1 - 4.0 * t2
    edge = 8.0 * t1 + t2
    p9 = t9 - 2.0 * t10
    p11 = t11 - 2.0 * t12
    r9 = t9 + t10
    r11 = t11 + t12
    out = [None] * 19
    out[0] = f[0] + 30.0 * t1 - 12.0 * t2

    def put(i, even, odd):
        out[i] = f[i] - (even + odd)
        out[i + 1] = f[i + 1] - (even - odd)

    put(1, axis + 2.0 * p9, -4.0 * t4)
    put(3, axis - p9 + p11, -4.0 * t6)
    put(5, axis - p9 - p11, -4.0 * t8)
    vxy, vxz, vyz = edge + r9 + r11, edge + r9 - r11, edge - 2.0 * r9
    put(7, vxy + t13, t4 + t6 + (t16 - t17))
    put(9, vxy - t13, t4 - t6 + (t16 + t17))
    put(11, vxz + t15, t4 + t8 - (t16 - t18))
    put(13, vxz - t15, t4 - t8 - (t16 + t18))
    put(15, vyz + t14, t6 + t8 + (t17 - t18))
    put(17, vyz - t14, t6 - t8 + (t17 + t18))
    return out


def collide_kernel(par, pops_hbm, shear_hbm, *refs):
    given, (post, near, far), held = refs[0:5], refs[5:8], refs[8:13]
    pops, sems = refs[13:]
    even = par[0] == 0
    rate_copy = pltpu.make_async_copy(shear_hbm, post.at[SHEAR], sems.at[4])
    rate_copy.start()
    copies = []
    for plane in range(2):
        for half in range(2):
            rows = slice(8 * half, 8 * half + 8)
            copy = pltpu.make_async_copy(
                pops_hbm.at[:, plane, rows, :], pops.at[:, plane, rows, :], sems.at[2 * plane + half]
            )
            copy.start()
            copies.append(copy)
    for n in range(5):
        copy = pltpu.make_async_copy(given[n], held[n], sems.at[5 + n])
        copy.start()
        copies.append(copy)
    rate_copy.wait()
    for plane in range(2):
        for half in range(2):
            rows = slice(8 * half, 8 * half + 8)
            copies[2 * plane + half].wait()
            rate = post[SHEAR, plane, rows, :]
            out = relax([pops[i, plane, rows, :] for i in range(19)], rate)
            for i in range(19):
                post[i, plane, rows, :] = out[i]

    for slot in range(20):
        up = post[X_LOW[slot][0], X_LOW[slot][1] + 2]
        down = post[X_HIGH[slot][0], X_HIGH[slot][1] - 2]
        near[slot] = jnp.where(even, up, down)
        far[slot] = jnp.where(even, down, up)
    for copy in copies[4:]:
        copy.wait()


def reader(par, post, near, far):
    even = par[0] == 0

    def main(q, rows=slice(0, 16)):
        if q < 20:
            return jnp.where(even, far[q, rows, :], near[q, rows, :])
        if q >= 60:
            return jnp.where(even, near[q - 60, rows, :], far[q - 60, rows, :])
        field, plane = PAIRS[q]
        return post[field, plane, rows, :]

    return main


def place_columns(tile, pairs, value_of, high, low):
    lane = lax.broadcasted_iota(jnp.int32, (16, 128), 1)
    for q in pairs:
        if (q < FIRST) == (tile == 0):
            slot = q - tile * FIRST
            value = value_of(q)
            mine = (lane >= 3 * slot) & (lane < 3 * slot + 3)
            high = jnp.where(mine, pltpu.roll(value, (3 * slot + 3) % 128, 1), high)
            low = jnp.where(mine, pltpu.roll(value, 3 * slot, 1), low)
    return high, low


def z_own_kernel(post, own):
    zero = jnp.zeros((16, 128), jnp.float32)
    for tile in range(2):
        own[0, tile], own[1, tile] = place_columns(
            tile, range(20, 60), lambda q: post[PAIRS[q][0], PAIRS[q][1]], zero, zero
        )


def z_pack_kernel(par, own, xnear, xfar, edge, near, far):
    main = reader(par, None, xnear, xfar)
    even = par[2] == 0
    lane = lax.broadcasted_iota(jnp.int32, (16, 128), 1)
    for tile in range(2):
        ghosts = (*range(20), *range(60, 80))
        high, low = place_columns(tile, ghosts, main, own[0, tile], own[1, tile])
        if tile == 1:
            sums = edge[...] + pltpu.roll(edge[...], 112, 1)
            odd = jnp.bitwise_and(lane - DEP_LANE, 1) == 1
            ours = (lane >= DEP_LANE) & (lane < DEP_LANE + 8)
            for shift in (DEP_LANE, DEP_LANE - 8):
                placed = pltpu.roll(sums, shift, 1)
                placed = jnp.where(odd, placed[16:32, :], placed[0:16, :])
                if shift == DEP_LANE:
                    high = jnp.where(ours, placed, high)
                else:
                    low = jnp.where(ours, placed, low)
        near[tile] = jnp.where(even, high, low)
        far[tile] = jnp.where(even, low, high)


def y_pack_kernel(par, post, xnear, xfar, znear, zfar, edge, near, far):
    main = reader(par, post, xnear, xfar)
    even = par[1] == 0
    even_z = par[2] == 0

    def put(row, count, high, low):
        near[row : row + count, :] = jnp.where(even, high, low)
        far[row : row + count, :] = jnp.where(even, low, high)

    top, bottom = slice(13, 16), slice(0, 3)
    for q in range(len(PAIRS)):
        put(3 * q, 3, main(q, top), main(q, bottom))
    put(240, 8, edge[0:8, :], edge[8:16, :])
    for tile in range(2):
        put(
            248 + 3 * tile,
            3,
            jnp.where(even_z, zfar[tile, top, :], znear[tile, top, :]),
            jnp.where(even_z, zfar[tile, bottom, :], znear[tile, bottom, :]),
        )
        put(
            254 + 3 * tile,
            3,
            jnp.where(even_z, znear[tile, top, :], zfar[tile, top, :]),
            jnp.where(even_z, znear[tile, bottom, :], zfar[tile, bottom, :]),
        )
    near[260:264, :] = jnp.zeros((4, 128), jnp.float32)
    far[260:264, :] = jnp.zeros((4, 128), jnp.float32)


def shifted(value, shift_y, shift_z):
    if shift_y:
        value = pltpu.roll(value, shift_y % 24, 0)
    if shift_z:
        value = pltpu.roll(value, shift_z % 256, 1)
    return value


def sided(first, second, tile):
    tile, slot = tile
    low = pltpu.roll(first[tile], (125 - 3 * slot) % 128, 1)
    high = pltpu.roll(second[tile], (-3 * slot) % 128, 1)
    lane = lax.broadcasted_iota(jnp.int32, low.shape, 1)
    return jnp.where(lane < 64, high, low)


def column_spot(q):
    return (0, q) if q < FIRST else (1, q - FIRST)


def collide_rows(rate_of, fields, plane, index):
    for z in range(2):
        lanes = slice(128 * z, 128 * z + 128)
        at = index + (slice(None), lanes)
        out = relax([fields[(i, plane) + at] for i in range(19)], rate_of(lanes))
        for i in range(19):
            fields[(i, plane) + at] = out[i]


def inner_kernel(par, post, xnear, xfar, znear, zfar, field_ext, second):
    main = reader(par, post, xnear, xfar)
    even_z = par[2] == 0
    low = [jnp.where(even_z, zfar[t], znear[t]) for t in range(2)]
    high = [jnp.where(even_z, znear[t], zfar[t]) for t in range(2)]
    for q in range(len(PAIRS)):
        field_ext[q, :, 0:128] = main(q)
        field_ext[q, :, 128:256] = sided(low, high, column_spot(q))
    for plane in range(4):
        for i in range(19):
            cx, cy, cz = SPEEDS[i]
            value = field_ext[INDEX[(i, plane - 1 - cx)]]
            if cy:
                value = pltpu.roll(value, cy % 16, 0)
            if cz:
                value = pltpu.roll(value, cz % 256, 1)
            second[i, plane] = value.reshape(2, 8, 256)
    for plane in range(4):
        rates = INDEX[(SHEAR, plane - 1)]

        def body(t, carry, plane=plane, rates=rates):
            row = pl.multiple_of(t * 8, 8)
            collide_rows(lambda lanes: field_ext[rates, pl.ds(row, 8), lanes], second, plane, (t,))
            return carry

        lax.fori_loop(0, 2, body, 0)


def step_kernel(
    par,
    field_ext,
    middle,
    znear,
    zfar,
    ynear,
    yfar,
    dep_a,
    dep_b,
    pops_out,
    fluid,
    partial,
    snear,
    sfar,
    window,
    rim,
):
    even_x, even_y, even_z = par[0] == 0, par[1] == 0, par[2] == 0

    def dep(c, k, plane):
        return (dep_a if c < 2 else dep_b)[c % 2, k, plane]

    def y_low(row, count):
        return jnp.where(even_y, yfar[row : row + count, :], ynear[row : row + count, :])

    def y_high(row, count):
        return jnp.where(even_y, ynear[row : row + count, :], yfar[row : row + count, :])

    pad = jnp.zeros((2, 128), jnp.float32)
    packed = [
        [
            jnp.concatenate([y_high(row, 3), y_low(row, 3), pad], 0)
            for row in (248 + 6 * side, 251 + 6 * side)
        ]
        for side in range(2)
    ]
    for q in range(len(PAIRS)):
        window[q, 0:8, :] = field_ext[q, 8:16, :]
        window[q, 8:11, 0:128] = y_high(3 * q, 3)
        window[q, 11:14, 0:128] = y_low(3 * q, 3)
        window[q, 8:14, 128:256] = sided(packed[0], packed[1], column_spot(q))[0:6, :]
        window[q, 14:16, :] = field_ext[q, 0:2, :]

    for plane in range(4):
        rates = INDEX[(SHEAR, plane - 1)]
        for i in range(19):
            cx, cy, cz = SPEEDS[i]
            value = window[INDEX[(i, plane - 1 - cx)], 7 - cy : 15 - cy, :]
            if cz:
                value = pltpu.roll(value, cz % 256, 1)
            rim[i, plane] = value
        collide_rows(lambda lanes, rates=rates: window[rates, 7:15, lanes], rim, plane, ())

    row_of = lax.broadcasted_iota(jnp.int32, (8, 256), 0)

    def collided(i, plane):
        down, up = pltpu.roll(rim[i, plane], 1, 0), pltpu.roll(rim[i, plane], 7, 0)
        return jnp.concatenate(
            [
                jnp.where(row_of == 0, down, middle[i, plane, 0]),
                jnp.where(row_of == 7, up, middle[i, plane, 1]),
                jnp.where(row_of < 4, up, down),
            ],
            0,
        )

    lane16 = lax.broadcasted_iota(jnp.int32, (16, 128), 1)
    row8 = lax.broadcasted_iota(jnp.int32, (8, 128), 0)
    totals = [[None, None] for _ in range(4)]
    ups, downs = [None] * 4, [None] * 4
    for plane in range(2):
        rho = jx = jy = jz = None

        def add(total, value, sign):
            if sign == 0:
                return total
            if total is None:
                return value if sign > 0 else -value
            return total + value if sign > 0 else total - value

        for i in range(19):
            cx, cy, cz = SPEEDS[i]
            value = shifted(collided(i, plane + 1 - cx), cy, cz)
            pops_out[i, plane] = value[0:16, 0:128]
            rho = add(rho, value, 1)
            jx, jy, jz = add(jx, value, cx), add(jy, value, cy), add(jz, value, cz)
        u = [jx / rho, jy / rho, jz / rho]
        for c in range(3):
            fluid[c, plane] = u[c][0:16, 0:128]

        def moved(k, speed):
            s = dep(3, k, plane)
            return [dep(c, k, plane) - speed[c] * s for c in range(3)] + [2.0 * s]

        inner = [u[c][0:16, 0:128] for c in range(3)]
        total = moved(0, inner)
        tops = moved(1, inner)
        bottoms = moved(2, inner)

        def y_ext(k):
            ghosts = []
            for c in range(4):
                row = 240 + 2 * c + plane
                if k == 3:
                    ghost = jnp.where(row8 == 7, jnp.broadcast_to(y_low(row, 1), (8, 128)), 0.0)
                else:
                    ghost = jnp.where(row8 == 0, jnp.broadcast_to(y_high(row, 1), (8, 128)), 0.0)
                ghosts.append(jnp.concatenate([dep(c, k, plane), ghost], 0))
            return ghosts

        def z_ext(k):
            ghosts = []
            for c in range(4):
                spot = DEP_LANE + 2 * c + plane
                if k == 5:
                    ghost = jnp.where(even_z, zfar[1], znear[1])
                    ghost = pltpu.roll(ghost, (127 - spot) % 128, 1)
                    ghost = jnp.where(lane16 == 127, ghost, 0.0)
                else:
                    ghost = jnp.where(even_z, znear[1], zfar[1])
                    ghost = pltpu.roll(ghost, (-spot) % 128, 1)
                    ghost = jnp.where(lane16 == 0, ghost, 0.0)
                ghosts.append(jnp.concatenate([dep(c, k, plane), ghost], 1))
            return ghosts

        for k, shift in ((3, 1), (4, 23)):
            v = y_ext(k)
            rows = [v[c] - jnp.where(v[3] != 0.0, u[c][:, 0:128] * v[3], 0.0) for c in range(3)]
            rows.append(2.0 * v[3])
            for c in range(4):
                total[c] = total[c] + pltpu.roll(rows[c], shift, 0)[0:16, :]
        for k, shift in ((5, 1), (6, 255)):
            v = z_ext(k)
            rows = [v[c] - jnp.where(v[3] != 0.0, u[c][0:16, :] * v[3], 0.0) for c in range(3)]
            rows.append(2.0 * v[3])
            for c in range(4):
                total[c] = total[c] + pltpu.roll(rows[c], shift, 1)[:, 0:128]
        for c in range(4):
            totals[c][plane] = total[c]
        if plane == 0:
            downs, held = bottoms, tops
        else:
            ups = tops
            for c in range(4):
                totals[c][0] = totals[c][0] + bottoms[c]
                totals[c][1] = totals[c][1] + held[c]
    for c in range(4):
        partial[c, 0] = totals[c][0]
        partial[c, 1] = totals[c][1]
        snear[c] = jnp.where(even_x, ups[c], downs[c])
        sfar[c] = jnp.where(even_x, downs[c], ups[c])


def pieces(value):
    coarse = value.astype(jnp.bfloat16)
    return coarse, (value - coarse.astype(jnp.float32)).astype(jnp.bfloat16)


def small(value):
    return value.astype(jnp.float32).astype(jnp.bfloat16)


def numbers(rows, width):
    return lax.broadcasted_iota(jnp.int32, (rows, width), 0)


BY_LANE = (((1,), (1,)), ((), ()))


def deposit_kernel(fields, cell, move, mask, mass, velocity, out, picked, keys):
    where = cell[...]
    width = where.shape[1]
    code = small(move[...] * 32 + jnp.right_shift(where, 7))
    spot = small(jnp.bitwise_and(where, 127))
    weight = 0.5 * mask[...].astype(jnp.float32) * mass[...]
    rows = small(numbers(256, width))
    keys[...] = jnp.where(rows == code, jnp.bfloat16(1), jnp.bfloat16(0))
    here = rows[0:128] == spot
    for n, c in enumerate(fields):
        value = weight * velocity[c : c + 1, :] if c < 3 else weight
        for piece, part in enumerate(pieces(value)):
            at = 256 * n + 128 * piece
            picked[at : at + 128, :] = jnp.where(here, part, jnp.bfloat16(0))
    total = lax.dot_general(
        keys[...], picked[...], BY_LANE, preferred_element_type=jnp.float32
    )
    for n in range(2):
        out[n] = total[:, 256 * n : 256 * n + 128] + total[:, 256 * n + 128 : 256 * n + 256]


def edge_rows(mask, mass, velocity, target, code):
    weight = 0.5 * mask[...].astype(jnp.float32) * mass[...]
    width = weight.shape[1]
    values = [weight * velocity[c : c + 1, :] for c in range(3)] + [weight]
    field = jnp.bitwise_and(jnp.right_shift(numbers(16, width), 1), 3)
    chosen = jnp.where(field == 0, values[0], values[1])
    chosen = jnp.where(field == 2, values[2], chosen)
    chosen = jnp.where(field == 3, values[3], chosen)
    chosen = jnp.where(code == target, chosen, 0.0)
    return jnp.concatenate(pieces(chosen), 0)


def z_edge_kernel(cell, move, mask, mass, velocity, out):
    where = cell[...]
    width = where.shape[1]
    low = jnp.right_shift(numbers(16, width), 3)
    target = jnp.where(low == 0, 5 * 128 + 127, 6 * 128)
    code = move[...] * 128 + jnp.bitwise_and(where, 127)
    rows = edge_rows(mask, mass, velocity, target, code)
    line = jnp.where(
        small(numbers(32, width)) == small(jnp.right_shift(where, 7)), jnp.bfloat16(1), jnp.bfloat16(0)
    )
    out[...] = jnp.zeros_like(out)
    out[:, 0:32] = lax.dot_general(line, rows, BY_LANE, preferred_element_type=jnp.float32)


def y_edge_kernel(cell, move, mask, mass, velocity, out, tall):
    where = cell[...]
    width = where.shape[1]
    row = numbers(16, width)
    plane = jnp.bitwise_and(row, 1) * 16
    target = jnp.where(row < 8, 3 * 32 + 15 + plane, 4 * 32 + plane)
    code = move[...] * 32 + jnp.right_shift(where, 7)
    rows = edge_rows(mask, mass, velocity, target, code)
    here = jnp.where(
        small(numbers(128, width)) == small(jnp.bitwise_and(where, 127)), jnp.bfloat16(1), jnp.bfloat16(0)
    )
    total = lax.dot_general(rows, here, BY_LANE, preferred_element_type=jnp.float32)
    out[...] = total[0:16, :] + total[16:32, :]
    for j in range(width // 128):
        for c in range(3):
            tall[c, j : j + 1, :] = velocity[c : c + 1, 128 * j : 128 * j + 128]


def drag_kernel(cell, mask, velocity, fluid, out):
    for group in range(8):
        rows = slice(8 * group, 8 * group + 8)
        where = cell[rows, :]
        lane = jnp.bitwise_and(where, 127)
        line = jnp.right_shift(where, 7)
        picked = [jnp.zeros((8, 128), jnp.float32) for _ in range(3)]
        for r in range(32):
            mine = line == r
            for c in range(3):
                table = jnp.broadcast_to(fluid[c, r : r + 1, :], (8, 128))
                value = jnp.take_along_axis(table, lane, axis=1)
                picked[c] = jnp.where(mine, value, picked[c])
        half = 0.5 * mask[rows, :].astype(jnp.float32)
        for c in range(3):
            old = velocity[c, rows, :]
            new = old + half * (picked[c] - old)
            for r in range(8):
                at = 128 * (8 * group + r)
                out[c : c + 1, at : at + 128] = new[r : r + 1, :]


def swap(value, axis, shifted_by_one):
    count = lax.axis_size(axis)
    pairs = []
    for i in range(count):
        if shifted_by_one:
            pairs.append((i, (i + 1) % count if i % 2 else (i - 1) % count))
        else:
            pairs.append((i, i ^ 1))
    return lax.ppermute(value, axis, pairs)


def both_swaps(near, far, axis):
    far = swap(far, axis, True)
    near = swap(near, axis, False)
    return near, far


def struct(*shape):
    return jax.ShapeDtypeStruct(shape, jnp.float32)


def call(kernel, outs, args, specs=None, scratch=(), flops=1000000, vmem=40):
    single = not isinstance(outs, tuple)
    return pl.pallas_call(
        kernel,
        out_shape=outs,
        in_specs=specs or [VMEM] * len(args),
        out_specs=VMEM if single else (VMEM,) * len(outs),
        scratch_shapes=scratch,
        compiler_params=pltpu.CompilerParams(vmem_limit_bytes=vmem << 20),
        cost_estimate=pl.CostEstimate(flops=flops, bytes_accessed=1000000, transcendentals=0),
    )(*args)


def body(populations, shear_rate, part_cell, part_move, part_mask, part_velocity, part_mass):
    par = jnp.stack([lax.axis_index(a) % 2 for a in ("gx", "gy", "gz")]).astype(jnp.int32)
    count = part_cell.shape[0]
    flat = (1, count)
    particles = (
        part_cell.reshape(flat),
        part_move.reshape(flat),
        part_mask.reshape(flat),
        part_mass.reshape(flat),
        part_velocity,
    )

    post, near, far, *particles = call(
        collide_kernel,
        (struct(20, 2, 16, 128), struct(20, 16, 128), struct(20, 16, 128))
        + tuple(jax.ShapeDtypeStruct(p.shape, p.dtype) for p in particles),
        (par,)
        + tuple(
            pltpu.with_memory_space_constraint(a, pltpu.HBM)
            for a in (populations, shear_rate, *particles)
        ),
        [SMEM] + [HBM] * 7,
        [pltpu.VMEM((19, 2, 16, 128), jnp.float32), pltpu.SemaphoreType.DMA((10,))],
    )
    xnear, xfar = both_swaps(near, far, "gx")

    edge = call(z_edge_kernel, struct(32, 128), particles)
    own = call(z_own_kernel, struct(2, 2, 16, 128), (post,))
    near, far = call(
        z_pack_kernel,
        (struct(2, 16, 128), struct(2, 16, 128)),
        (par, own, xnear, xfar, edge),
        [SMEM] + [VMEM] * 4,
    )
    znear, zfar = both_swaps(near, far, "gz")

    edge, velocity_tall = call(
        y_edge_kernel, (struct(16, 128), struct(3, count // 128, 128)), particles
    )
    scratch = [pltpu.VMEM((512, count), jnp.bfloat16), pltpu.VMEM((256, count), jnp.bfloat16)]
    deposits = [
        call(
            functools.partial(deposit_kernel, fields),
            struct(2, 256, 128),
            particles,
            scratch=scratch,
            flops=2000000000,
        ).reshape(2, 8, 2, 16, 128)
        for fields in ((0, 1), (2, 3))
    ]
    near, far = call(
        y_pack_kernel,
        (struct(Y_ROWS, 128), struct(Y_ROWS, 128)),
        (par, post, xnear, xfar, znear, zfar, edge),
        [SMEM] + [VMEM] * 6,
    )
    ynear, yfar = both_swaps(near, far, "gy")

    field_ext, inner = call(
        inner_kernel,
        (struct(len(PAIRS), 16, 256), struct(19, 4, 2, 8, 256)),
        (par, post, xnear, xfar, znear, zfar),
        [SMEM] + [VMEM] * 5,
        flops=20000000,
    )
    populations_out, fluid, partial, near, far = call(
        step_kernel,
        (
            struct(19, 2, 16, 128),
            struct(3, 2, 16, 128),
            struct(4, 2, 16, 128),
            struct(4, 16, 128),
            struct(4, 16, 128),
        ),
        (par, field_ext, inner, znear, zfar, ynear, yfar, *deposits),
        [SMEM] + [VMEM] * 8,
        [
            pltpu.VMEM((len(PAIRS), 16, 256), jnp.float32),
            pltpu.VMEM((19, 4, 8, 256), jnp.float32),
        ],
        flops=20000000,
    )
    snear, sfar = both_swaps(near, far, "gx")

    tall = (count // 128, 128)
    velocity_out = call(
        drag_kernel,
        struct(3, count),
        (
            particles[0].reshape(tall),
            particles[2].reshape(tall),
            velocity_tall,
            fluid.reshape(3, 32, 128),
        ),
    )

    even = par[0] == 0
    upper = lax.broadcasted_iota(jnp.int32, partial.shape, 1) == 1
    sources = partial + jnp.where(upper == even, snear[:, None], sfar[:, None])
    return populations_out, sources, velocity_out


def solution(mesh):
    placed = (
        P(None, "gx", "gy", "gz"),
        P("gx", "gy", "gz"),
        P(("gx", "gy", "gz")),
        P(("gx", "gy", "gz")),
        P(("gx", "gy", "gz")),
        P(None, ("gx", "gy", "gz")),
        P(("gx", "gy", "gz")),
    )
    return jax.shard_map(
        body,
        mesh=mesh,
        in_specs=placed,
        out_specs=(
            P(None, "gx", "gy", "gz"),
            P(None, "gx", "gy", "gz"),
            P(None, ("gx", "gy", "gz")),
        ),
        check_vma=False,
    )
```
